256 devices in a mesh: inst: 4 (over y_hi, core), elem: 64 (over x, y_lo, z).
Axes of the slice: x: 4, y: 4 (y_hi: 2, y_lo: 2; y = y_hi * 2 + y_lo), z: 8, core: 2. Of those that a mesh axis runs over, the one named last changes fastest.
Arguments:
- flow_state: float32 [8, 5, 125, 8192], P('inst', None, None, 'elem'), may hold values from -6 to 6
- flux_matrices: float32 [3, 5, 5], replicated, may hold values from -2.5 to 2.5
- derivative: float32 [3, 125, 125], replicated, may hold values from -0.5 to 0.5
- penalty: float32 [6, 5, 5], replicated, may hold values from -2.5 to 2.5
- lift_matrices: float32 [6, 125, 25], replicated, may hold values from -1.25 to 1.25
- frequency: float32 [1], replicated, may hold values from 0.5 to 2
- step_size: float32 [8192], P('elem'), may hold values from 0.05 to 0.3
- partner: int32 [8, 256], P(None, 'elem'), may hold values from 0 to 255, as said below
Outputs:
- new_state: float32 [8, 5, 125, 8192], P('inst', None, None, 'elem')
The draws below stay inside these ranges and needn't reach their ends.
Inputs may be any that keep to these rules, and one draw needn't show every extreme that they name: For each instance t there is one whole number o_t of 0 to 63 with partner[t, p * 4 + s] = ((p + o_t) mod 64) * 4 + s for every p and s.
All inputs are finite; a program needn't handle non-finite values.
Results may differ from the reference program's by a relative error of at most 0.0003.
Values sent between devices are 32-bit elements; how exact they have to be, the bound alone decides.
A program may use at most 64 MiB of HBM per device.

```python
import math
import jax
import jax.numpy as jnp
from jax import lax

NT = 8
VARS = 5
NODES = 125
FACE_NODES = 25
NSTR = 32
NSPAN = 4
NPITCH = 64
ELEMS = 8192


def draw_partner(key, part):
    offsets = jax.random.randint(jax.random.fold_in(key, 7), (NT,), 0, NPITCH)
    pitch_rows = jnp.arange(NPITCH)
    span_rows = jnp.arange(NSPAN)
    target = ((pitch_rows[None, :] + offsets[:, None]) % NPITCH)[:, :, None] * NSPAN + span_rows[None, None, :]
    return target.reshape(NT, NPITCH * NSPAN).astype(jnp.int32)


def levels(key, dims, cuts, low, largest):
    level = 1.0
    for position, blocks in cuts:
        draws = jax.random.uniform(jax.random.fold_in(jax.random.fold_in(key, 6), position), (blocks,), jnp.float32, low / len(cuts), largest / len(cuts))
        level = level * jnp.repeat(jnp.exp(draws), dims[position] // blocks).reshape((-1,) + (1,) * (len(dims) - 1 - position))
    return level


def centred(own_key, dims, spread, most, pieces=(), held_as=jnp.bfloat16):
    factor_of = levels(own_key, dims, pieces, -0.22, 0.18) if pieces else 1.0
    values = jax.random.normal(own_key, dims, jnp.float32) * spread * factor_of
    return jnp.minimum(jnp.maximum(values, -most), most).astype(held_as)


def setup_inputs(seed: int = 0) -> dict:
    splits = jax.random.split(jax.random.key(seed), 9)
    flow_state = centred(splits[0], (NT, VARS, NODES, ELEMS), 1.0, 6.0, ((0, 4), (3, 64)), jnp.float32)
    flux_matrices = centred(splits[1], (3, VARS, VARS), VARS ** -0.5, 2.5, (), jnp.float32)
    derivative = centred(splits[2], (3, NODES, NODES), NODES ** -0.5, 0.5, (), jnp.float32)
    penalty = centred(splits[3], (6, VARS, VARS), VARS ** -0.5, 2.5, (), jnp.float32)
    lift_matrices = centred(splits[4], (6, NODES, FACE_NODES), FACE_NODES ** -0.5, 1.25, (), jnp.float32)
    frequency = jnp.clip(jnp.exp(jax.random.uniform(splits[5], (1,), jnp.float32, math.log(0.5), math.log(2.0))), 0.5, 2.0)
    step_size = jnp.clip(jnp.exp(math.log(0.3) - 1.7917595 * jax.random.uniform(splits[6], (ELEMS,), jnp.float32) ** levels(splits[6], (ELEMS,), ((0, 64),), -0.2, 0.2)), 0.05, 0.3)
    partner = draw_partner(jax.random.fold_in(splits[8], 71), 0)
    return {"flow_state": flow_state, "flux_matrices": flux_matrices, "derivative": derivative, "penalty": penalty, "lift_matrices": lift_matrices, "frequency": frequency, "step_size": step_size, "partner": partner}


SECTION_WEIGHTS = (0.25, 1.0 / 3.0, 0.5, 1.0)
HIGHEST = lax.Precision.HIGHEST


def spectral_matrix(instances, frequency):
    ordinal = jnp.arange(instances)
    offset_pairs = ordinal[:, None] - ordinal[None, :]
    angles = jnp.pi * offset_pairs.astype(jnp.float32) / instances
    parity = (1 - 2 * (offset_pairs % 2)).astype(jnp.float32)
    on_diagonal = offset_pairs == 0
    sine_values = jnp.where(on_diagonal, 1.0, jnp.sin(angles))
    return jnp.where(on_diagonal, 0.0, 0.5 * parity * jnp.cos(angles) / sine_values) * frequency


def spatial_one(current, partner_row, flux_matrices, derivative, penalty, lift_matrices):
    volume = jnp.zeros_like(current)
    for direction in range(3):
        mixed = jnp.einsum('ab,bne->ane', flux_matrices[direction], current, precision=HIGHEST)
        volume = volume + jnp.einsum('mn,ane->ame', derivative[direction], mixed, precision=HIGHEST)
    lattice = current.reshape(VARS, 5, 5, 5, -1)
    picked = [lattice[:, 0], lattice[:, 4], lattice[:, :, 0], lattice[:, :, 4], lattice[:, :, :, 0], lattice[:, :, :, 4]]
    surfaces = [surface.reshape(VARS, FACE_NODES, NPITCH, NSPAN, NSTR) for surface in picked]
    half_way = NSTR // 2
    rotor_slab = surfaces[1][..., half_way - 1].reshape(VARS, FACE_NODES, NPITCH * NSPAN)
    stator_slab = surfaces[0][..., half_way].reshape(VARS, FACE_NODES, NPITCH * NSPAN)
    rotor_seen = rotor_slab[:, :, partner_row].reshape(VARS, FACE_NODES, NPITCH, NSPAN)
    inverse = jnp.argsort(partner_row)
    stator_seen = stator_slab[:, :, inverse].reshape(VARS, FACE_NODES, NPITCH, NSPAN)
    zero_column = jnp.zeros_like(surfaces[0][..., :1])
    west_side = jnp.concatenate([zero_column, surfaces[1][..., :-1]], -1).at[..., half_way].set(rotor_seen)
    east_side = jnp.concatenate([surfaces[0][..., 1:], zero_column], -1).at[..., half_way - 1].set(stator_seen)
    south_side = jnp.roll(surfaces[3], 1, axis=2)
    north_side = jnp.roll(surfaces[2], -1, axis=2)
    zero_row = jnp.zeros_like(surfaces[0][:, :, :, :1])
    floor_side = jnp.concatenate([zero_row, surfaces[5][:, :, :, :-1]], 3)
    ceiling_side = jnp.concatenate([surfaces[4][:, :, :, 1:], zero_row], 3)
    neighbours = [west_side, east_side, south_side, north_side, floor_side, ceiling_side]
    total = volume
    for face_index in range(6):
        jump = (neighbours[face_index] - surfaces[face_index]).reshape(VARS, FACE_NODES, -1)
        flux_jump = jnp.einsum('ab,bne->ane', penalty[face_index], jump, precision=HIGHEST)
        total = total + jnp.einsum('mn,ane->ame', lift_matrices[face_index], flux_jump, precision=HIGHEST)
    return total


def reference(flow_state, flux_matrices, derivative, penalty, lift_matrices, frequency, step_size, partner):
    spectral = spectral_matrix(NT, frequency[0])

    def one_instance(members):
        return spatial_one(members[0], members[1], flux_matrices, derivative, penalty, lift_matrices)

    def section_residual(current):
        spatial = lax.map(one_instance, (current, partner))
        return jnp.einsum('ts,svne->tvne', spectral, current, precision=HIGHEST) + spatial

    current = flow_state
    for weight in SECTION_WEIGHTS:
        current = flow_state - weight * step_size * section_residual(current)
    return current
```

```python
import math

import jax
import jax.numpy as jnp
from jax import lax
from jax.experimental import pallas as pl
from jax.experimental.pallas import tpu as pltpu
from jax.sharding import PartitionSpec as P

MESH = pl.DeviceIdType.MESH
F32 = jnp.float32
BF16 = jnp.bfloat16
HIGHEST = lax.Precision.HIGHEST

STAGES = 4
INST = 4
RING = 8
ROWS = 640
HALF = ROWS // 2
LANES = 128
STREAM = 32
FACE = 25


def split(value):
    high = value.astype(BF16)
    low = (value - high.astype(F32)).astype(BF16)
    return high, low


def kernel(
    flow_ref, flux_ref, derivative_ref, penalty_ref, lift_ref, frequency_ref, step_ref, partner_ref,
    out_ref,
    x_ref, a_send, a_recv, b_send, b_recv, base_ref, u_ref, ru_ref, wk_ref, wa_ref, wb_ref, ra_ref, rb_ref,
    sh_ref, sl_ref, r_ref, tr_send, tr_recv, t01_ref, zbuf, hbuf, dp_ref, lt_ref, pb_ref, ct_ref,
    io_sem, as_sem, ar_sem, bs_sem, br_sem, ts_sem, tr_sem, zs_sem, zr_sem, hs_sem, hr_sem, own_sem,
):
    inst = lax.axis_index("inst")
    row = lax.axis_index("elem")
    rows_total = lax.axis_size("elem")
    low = lax.rem(row, RING)
    high = lax.div(row, RING)
    north = lax.rem(row + 1, rows_total)
    south = lax.rem(row + rows_total - 1, rows_total)

    def inst_peer(distance):
        return lax.rem(inst + distance, INST)

    def low_peer(distance):
        return lax.rem(low + distance, RING)

    def high_peer(distance):
        return lax.rem(high + distance, RING)

    loads = [
        pltpu.make_async_copy(
            flow_ref.at[half, var], x_ref.at[half, pl.ds(var * 128, 125), :], io_sem.at[half * 5 + var]
        )
        for half in range(2)
        for var in range(5)
    ]
    for load in loads:
        load.start()

    tr_recv[...] = jnp.zeros_like(tr_recv)

    barrier = pltpu.get_barrier_semaphore()
    for distance in range(1, INST):
        pl.semaphore_signal(barrier, inc=1, device_id=(inst_peer(distance), row), device_id_type=MESH)
    for other in (north, south):
        pl.semaphore_signal(barrier, inc=1, device_id=(inst, other), device_id_type=MESH)
    for distance in range(1, RING):
        pl.semaphore_signal(
            barrier, inc=1, device_id=(inst, high * RING + low_peer(distance)), device_id_type=MESH
        )
        pl.semaphore_signal(
            barrier, inc=1, device_id=(inst, high_peer(distance) * RING + low), device_id_type=MESH
        )

    lane = lax.broadcasted_iota(jnp.int32, (1, LANES), 1)

    for load in loads:
        load.wait()
    for half in range(2):
        for var in range(5):
            x_ref[half, var * 128 + 125 : var * 128 + 128, :] = jnp.zeros((3, LANES), F32)
    chunk = 40

    def pack(step, carry):
        start = pl.multiple_of(step * chunk, 8)
        parts = [
            x_ref[quarter % 2, pl.ds((quarter // 2) * HALF + start, chunk), :] for quarter in range(4)
        ]
        for target in range(INST):
            packed = None
            for quarter in range(4):
                turn = (STREAM * (quarter - target)) % LANES
                moved = parts[quarter] if turn == 0 else pltpu.roll(parts[quarter], turn, 1)
                packed = moved if packed is None else jnp.where(lane >= STREAM * quarter, moved, packed)
            a_send[target, pl.ds(start, chunk), :] = packed
        return carry

    lax.fori_loop(0, HALF // chunk, pack, 0)

    pl.semaphore_wait(barrier, INST - 1 + 2 + 2 * (RING - 1))

    def exchange(send_buffer, recv_buffer, send_sem, recv_sem, distance):
        peer = inst_peer(distance)
        return pltpu.make_async_remote_copy(
            src_ref=send_buffer.at[peer],
            dst_ref=recv_buffer.at[inst],
            send_sem=send_sem.at[peer],
            recv_sem=recv_sem.at[inst],
            device_id=(peer, row),
            device_id_type=MESH,
        )

    def arrival(recv_buffer, send_buffer, send_sem, recv_sem, distance):
        peer = inst_peer(distance)
        return pltpu.make_async_remote_copy(
            src_ref=send_buffer.at[peer],
            dst_ref=recv_buffer.at[peer],
            send_sem=send_sem.at[peer],
            recv_sem=recv_sem.at[peer],
            device_id=(peer, row),
            device_id_type=MESH,
        )

    for distance in (2, 3, 1):
        exchange(a_send, a_recv, as_sem, ar_sem, distance).start()
    own = pltpu.make_async_copy(a_send.at[inst], a_recv.at[inst], own_sem)
    own.start()

    dp_ref[...] = jnp.zeros_like(dp_ref)
    for direction in range(3):
        dp_ref[direction, 0:125, 0:125] = derivative_ref[direction]

    def volume(var, carry):
        start = pl.multiple_of(var * 128, 128)
        for other in range(5):
            block = flux_ref[0, var, other] * dp_ref[0]
            block = block + flux_ref[1, var, other] * dp_ref[1]
            block = block + flux_ref[2, var, other] * dp_ref[2]
            fine, rest = split(block)
            wk_ref[pl.ds(start, 128), other * 128 : (other + 1) * 128] = fine
            wk_ref[pl.ds(start, 128), ROWS + other * 128 : ROWS + (other + 1) * 128] = fine
            wk_ref[pl.ds(start, 128), 2 * ROWS + other * 128 : 2 * ROWS + (other + 1) * 128] = rest
        return carry

    lax.fori_loop(0, 5, volume, 0)

    face_column = lax.broadcasted_iota(jnp.int32, (FACE, LANES), 1)
    face_row = lax.broadcasted_iota(jnp.int32, (FACE, LANES), 0)
    repeat = ((lax.rem(face_column, FACE) == face_row) & (face_column < 125)).astype(F32)
    var_column = lax.broadcasted_iota(jnp.int32, (5, LANES), 1)
    var_row = lax.broadcasted_iota(jnp.int32, (5, LANES), 0)
    spread = (lax.div(var_column, FACE) == var_row).astype(F32)
    lt_ref[...] = jnp.zeros_like(lt_ref)
    for face in range(6):
        lt_ref[face, 0:125, :] = jnp.dot(
            lift_ref[face], repeat, precision=HIGHEST, preferred_element_type=F32
        )
        pb_ref[face, 0:5, :] = jnp.dot(
            penalty_ref[face], spread, precision=HIGHEST, preferred_element_type=F32
        )
        target, place, width = (wb_ref, face, 256) if face < 2 else (wa_ref, face - 2, 512)
        for var in range(5):
            fine, rest = split(lt_ref[face] * pb_ref[face, var : var + 1, :])
            here = slice(var * 128, (var + 1) * 128)
            target[here, place * 128 : (place + 1) * 128] = fine
            target[here, width + place * 128 : width + (place + 1) * 128] = fine
            target[here, 2 * width + place * 128 : 2 * width + (place + 1) * 128] = rest

    to_lane = lax.broadcasted_iota(jnp.int32, (256, 256), 1)
    from_lane = lax.broadcasted_iota(jnp.int32, (256, 256), 0)
    apart = to_lane - from_lane
    turns = lax.shift_right_arithmetic(apart, 5) & 7
    aligned = (apart & 31) == 0
    spectral = jnp.zeros((256, 256), F32)
    for turn in range(1, 8):
        if turn != 4:
            weight = 0.5 * (-1) ** turn / math.tan(math.pi * turn / 8)
            spectral = jnp.where(aligned & (turns == turn), weight, spectral)
    spectral = spectral * frequency_ref[0]
    fine, rest = split(spectral)
    sh_ref[...] = fine
    sl_ref[...] = rest

    first = pltpu.roll(step_ref[...], lax.rem((INST - inst) * STREAM, LANES), 1)
    first = jnp.where(lane < STREAM, first, 0.0)
    step_lane = first + pltpu.roll(first, 32, 1) + pltpu.roll(first, 64, 1) + pltpu.roll(first, 96, 1)

    ahead = lax.shift_right_arithmetic(jnp.broadcast_to(partner_ref[:, 0:1], (8, LANES)), 2)
    behind = (2 * row + 128 - ahead) & 63

    t01_ref[...] = jnp.zeros_like(t01_ref)
    ct_ref[...] = jnp.zeros_like(ct_ref)
    tr_send[...] = jnp.zeros_like(tr_send)

    own.wait()
    for distance in (1, 2, 3):
        arrival(a_recv, a_send, as_sem, ar_sem, distance).wait_recv()

    for side in range(2):
        def unpack(step, carry, side=side):
            start = pl.multiple_of(step * chunk, 8)
            even = a_recv[2 * side, pl.ds(start, chunk), :]
            odd = a_recv[2 * side + 1, pl.ds(start, chunk), :]
            upper = jnp.where(lane < 64, even, pltpu.roll(odd, 64, 1))
            lower = jnp.where(lane < 64, pltpu.roll(even, 64, 1), odd)
            base_ref[side, pl.ds(start, chunk), :] = upper
            u_ref[side, pl.ds(start, chunk), :] = upper
            base_ref[side, pl.ds(HALF + start, chunk), :] = lower
            u_ref[side, pl.ds(HALF + start, chunk), :] = lower
            return carry

        lax.fori_loop(0, HALF // chunk, unpack, 0)

    stream = lane & 31

    def low_copy(k, distance, sender):
        return pltpu.make_async_remote_copy(
            src_ref=zbuf.at[k, sender],
            dst_ref=zbuf.at[k, sender],
            send_sem=zs_sem.at[k, distance],
            recv_sem=zr_sem.at[k, sender],
            device_id=(inst, high * RING + low_peer(distance)),
            device_id_type=MESH,
        )

    def high_copy(k, distance, sender):
        return pltpu.make_async_remote_copy(
            src_ref=hbuf.at[k, sender],
            dst_ref=hbuf.at[k, sender],
            send_sem=hs_sem.at[k, distance],
            recv_sem=hr_sem.at[k, sender],
            device_id=(inst, high_peer(distance) * RING + low),
            device_id_type=MESH,
        )

    def trace_copy(k, sent, landed, device):
        return pltpu.make_async_remote_copy(
            src_ref=tr_send.at[k, sent],
            dst_ref=tr_recv.at[k, landed],
            send_sem=ts_sem.at[k, sent],
            recv_sem=tr_sem.at[k, landed],
            device_id=device,
            device_id_type=MESH,
        )

    def northward(k):
        return trace_copy(k, 1, 0, (inst, north))

    def southward(k):
        return trace_copy(k, 0, 1, (inst, south))

    def upward(k):
        return trace_copy(k, 3, 2, (lax.rem(inst + 1, INST), row))

    def downward(k):
        return trace_copy(k, 2, 3, (lax.rem(inst + INST - 1, INST), row))

    has_above = inst < INST - 1
    has_below = inst > 0

    def stage(k, carry):
        weight = jnp.where(k == 0, 0.25, jnp.where(k == 1, 1.0 / 3.0, jnp.where(k == 2, 0.5, 1.0)))
        for side in range(2):
            for var in range(5):
                t01_ref[0, side, var * 25 : var * 25 + 25, :] = u_ref[side, var * 128 : var * 128 + 25, :]
                t01_ref[1, side, var * 25 : var * 25 + 25, :] = u_ref[
                    side, var * 128 + 100 : var * 128 + 125, :
                ]
        mixed = jnp.where(
            stream == 15,
            t01_ref[1, 0],
            jnp.where(
                stream == 16,
                t01_ref[0, 0],
                jnp.where(stream == 17, pltpu.roll(t01_ref[1, 1], 2, 1), pltpu.roll(t01_ref[0, 1], 2, 1)),
            ),
        )
        ct_ref[0] = jnp.transpose(mixed)
        zbuf[k, low, 0, 0:4, :] = ct_ref[0, pl.ds(15, 4, stride=32), :]
        zbuf[k, low, 0, 4:8, :] = ct_ref[0, pl.ds(17, 4, stride=32), :]
        zbuf[k, low, 1, 0:4, :] = ct_ref[0, pl.ds(16, 4, stride=32), :]
        zbuf[k, low, 1, 4:8, :] = ct_ref[0, pl.ds(18, 4, stride=32), :]
        for distance in (4, 3, 5, 2, 6, 1, 7):
            low_copy(k, distance, low).start()

        for side in range(2):
            for var in range(5):
                for depth in range(5):
                    tr_send[k, 0, side, pl.ds(var * 25 + depth, 5, stride=5), :] = u_ref[
                        side, pl.ds(var * 128 + depth, 5, stride=25), :
                    ]
                    tr_send[k, 1, side, pl.ds(var * 25 + depth, 5, stride=5), :] = u_ref[
                        side, pl.ds(var * 128 + 20 + depth, 5, stride=25), :
                    ]
        northward(k).start()
        southward(k).start()
        for side in range(2):
            for var in range(5):
                tr_send[k, 2, side, var * 25 : var * 25 + 25, :] = u_ref[
                    side, pl.ds(var * 128, 25, stride=5), :
                ]
                tr_send[k, 3, side, var * 25 : var * 25 + 25, :] = u_ref[
                    side, pl.ds(var * 128 + 4, 25, stride=5), :
                ]

        @pl.when(has_above)
        def _():
            upward(k).start()

        @pl.when(has_below)
        def _():
            downward(k).start()

        for side in range(2):
            here = slice(side * LANES, (side + 1) * LANES)
            fine, rest = split(u_ref[side])
            ru_ref[0:ROWS, here] = fine
            ru_ref[ROWS : 2 * ROWS, here] = rest
            ru_ref[2 * ROWS : 3 * ROWS, here] = fine
        r_ref[...] = jnp.dot(wk_ref[...], ru_ref[...], preferred_element_type=F32)
        r_ref[...] += jnp.dot(ru_ref[0:ROWS, :], sh_ref[...], preferred_element_type=F32)
        r_ref[...] += jnp.dot(ru_ref[ROWS : 2 * ROWS, :], sh_ref[...], preferred_element_type=F32)
        r_ref[...] += jnp.dot(ru_ref[0:ROWS, :], sl_ref[...], preferred_element_type=F32)

        for distance in range(1, RING):
            low_copy(k, distance, low_peer(distance)).wait_recv()
        rotor = zbuf[k, 0, 0]
        stator = zbuf[k, 0, 1]
        for other in range(1, RING):
            rotor = jnp.where((ahead & 7) == other, zbuf[k, other, 0], rotor)
            stator = jnp.where((behind & 7) == other, zbuf[k, other, 1], stator)
        hbuf[k, high, 0] = rotor
        hbuf[k, high, 1] = stator
        for distance in (3, 5, 2, 6, 1, 7, 4):
            high_copy(k, distance, high).start()

        northward(k).wait_recv()
        southward(k).wait_recv()

        @pl.when(has_below)
        def _():
            upward(k).wait_recv()

        @pl.when(has_above)
        def _():
            downward(k).wait_recv()

        for face in range(4):
            for side in range(2):
                here = slice(side * LANES, (side + 1) * LANES)
                fine, rest = split(tr_recv[k, face, side] - tr_send[k, face, side])
                ra_ref[face * 128 : (face + 1) * 128, here] = fine
                ra_ref[512 + face * 128 : 512 + (face + 1) * 128, here] = rest
                ra_ref[1024 + face * 128 : 1024 + (face + 1) * 128, here] = fine
        r_ref[...] += jnp.dot(wa_ref[...], ra_ref[...], preferred_element_type=F32)

        for distance in range(1, RING):
            high_copy(k, distance, high_peer(distance)).wait_recv()
        rotor = hbuf[k, 0, 0]
        stator = hbuf[k, 0, 1]
        for other in range(1, RING):
            rotor = jnp.where(lax.shift_right_arithmetic(ahead, 3) == other, hbuf[k, other, 0], rotor)
            stator = jnp.where(lax.shift_right_arithmetic(behind, 3) == other, hbuf[k, other, 1], stator)
        ct_ref[1, pl.ds(16, 4, stride=32), :] = rotor[0:4]
        ct_ref[1, pl.ds(14, 4, stride=32), :] = rotor[4:8]
        ct_ref[1, pl.ds(15, 4, stride=32), :] = stator[0:4]
        ct_ref[1, pl.ds(13, 4, stride=32), :] = stator[4:8]
        seen = jnp.transpose(ct_ref[1])
        for side in range(2):
            here = slice(side * LANES, (side + 1) * LANES)
            across = seen if side == 0 else pltpu.roll(seen, 2, 1)
            west = jnp.where(stream == 0, 0.0, pltpu.roll(t01_ref[1, side], 1, 1))
            west = jnp.where(stream == 16, across, west)
            east = jnp.where(stream == 31, 0.0, pltpu.roll(t01_ref[0, side], 127, 1))
            east = jnp.where(stream == 15, across, east)
            for face, value in ((0, west), (1, east)):
                fine, rest = split(value - t01_ref[face, side])
                rb_ref[face * 128 : (face + 1) * 128, here] = fine
                rb_ref[256 + face * 128 : 256 + (face + 1) * 128, here] = rest
                rb_ref[512 + face * 128 : 512 + (face + 1) * 128, here] = fine
        r_ref[...] += jnp.dot(wb_ref[...], rb_ref[...], preferred_element_type=F32)
        scale = weight * step_lane
        for side in range(2):
            u_ref[side] = base_ref[side] - scale * r_ref[:, side * LANES : (side + 1) * LANES]

        northward(k).wait_send()
        southward(k).wait_send()

        @pl.when(has_above)
        def _():
            upward(k).wait_send()

        @pl.when(has_below)
        def _():
            downward(k).wait_send()

        for distance in range(1, RING):
            low_copy(k, distance, low).wait_send()
            high_copy(k, distance, high).wait_send()
        return carry

    lax.fori_loop(0, STAGES, stage, 0)

    for target in range(INST):
        def repack(step, carry, target=target):
            start = pl.multiple_of(step * chunk, 8)
            upper = u_ref[target // 2, pl.ds(start, chunk), :]
            lower = u_ref[target // 2, pl.ds(HALF + start, chunk), :]
            if target % 2 == 0:
                packed = jnp.where(lane < 64, upper, pltpu.roll(lower, 64, 1))
            else:
                packed = jnp.where(lane < 64, pltpu.roll(upper, 64, 1), lower)
            b_send[target, pl.ds(start, chunk), :] = packed
            return carry

        lax.fori_loop(0, HALF // chunk, repack, 0)
    for distance in (2, 3, 1):
        exchange(b_send, b_recv, bs_sem, br_sem, distance).start()
    own = pltpu.make_async_copy(b_send.at[inst], b_recv.at[inst], own_sem)
    own.start()
    for distance in range(1, INST):
        exchange(a_send, a_recv, as_sem, ar_sem, distance).wait_send()
    own.wait()
    for distance in (1, 2, 3):
        arrival(b_recv, b_send, bs_sem, br_sem, distance).wait_recv()

    def deliver(step, carry):
        start = pl.multiple_of(step * chunk, 8)
        parts = [b_recv[source, pl.ds(start, chunk), :] for source in range(INST)]
        for quarter in range(4):
            whole = None
            for source in range(INST):
                turn = (STREAM * (source - quarter)) % LANES
                moved = parts[source] if turn == 0 else pltpu.roll(parts[source], turn, 1)
                whole = moved if whole is None else jnp.where(lane >= STREAM * source, moved, whole)
            x_ref[quarter % 2, pl.ds((quarter // 2) * HALF + start, chunk), :] = whole
        return carry

    lax.fori_loop(0, HALF // chunk, deliver, 0)
    stores = [
        pltpu.make_async_copy(
            x_ref.at[half, pl.ds(var * 128, 125), :], out_ref.at[half, var], io_sem.at[half * 5 + var]
        )
        for half in range(2)
        for var in range(5)
    ]
    for store in stores:
        store.start()
    for distance in range(1, INST):
        exchange(b_send, b_recv, bs_sem, br_sem, distance).wait_send()
    for store in stores:
        store.wait()


def per_device(
    flow_state, flux_matrices, derivative, penalty, lift_matrices, frequency, step_size, partner
):
    anywhere = pl.BlockSpec(memory_space=pl.ANY)
    vector = pl.BlockSpec(memory_space=pltpu.VMEM)
    scalar = pl.BlockSpec(memory_space=pltpu.SMEM)
    dma = pltpu.SemaphoreType.DMA
    return pl.pallas_call(
        kernel,
        out_shape=jax.ShapeDtypeStruct(flow_state.shape, F32),
        in_specs=[anywhere, scalar, vector, vector, vector, scalar, vector, vector],
        out_specs=anywhere,
        scratch_shapes=[
            pltpu.VMEM((2, ROWS, LANES), F32),
            pltpu.VMEM((INST, HALF, LANES), F32),
            pltpu.VMEM((INST, HALF, LANES), F32),
            pltpu.VMEM((INST, HALF, LANES), F32),
            pltpu.VMEM((INST, HALF, LANES), F32),
            pltpu.VMEM((2, ROWS, LANES), F32),
            pltpu.VMEM((2, ROWS, LANES), F32),
            pltpu.VMEM((3 * ROWS, 256), BF16),
            pltpu.VMEM((ROWS, 3 * ROWS), BF16),
            pltpu.VMEM((ROWS, 3 * 512), BF16),
            pltpu.VMEM((ROWS, 3 * 256), BF16),
            pltpu.VMEM((3 * 512, 256), BF16),
            pltpu.VMEM((3 * 256, 256), BF16),
            pltpu.VMEM((256, 256), BF16),
            pltpu.VMEM((256, 256), BF16),
            pltpu.VMEM((ROWS, 256), F32),
            pltpu.VMEM((STAGES, 4, 2, LANES, LANES), F32),
            pltpu.VMEM((STAGES, 4, 2, LANES, LANES), F32),
            pltpu.VMEM((2, 2, LANES, LANES), F32),
            pltpu.VMEM((STAGES, RING, 2, 8, LANES), F32),
            pltpu.VMEM((STAGES, RING, 2, 8, LANES), F32),
            pltpu.VMEM((3, LANES, LANES), F32),
            pltpu.VMEM((6, LANES, LANES), F32),
            pltpu.VMEM((6, 8, LANES), F32),
            pltpu.VMEM((2, LANES, LANES), F32),
            dma((10,)),
            dma((INST,)),
            dma((INST,)),
            dma((INST,)),
            dma((INST,)),
            dma((STAGES, 4)),
            dma((STAGES, 4)),
            dma((STAGES, RING)),
            dma((STAGES, RING)),
            dma((STAGES, RING)),
            dma((STAGES, RING)),
            dma,
        ],
        compiler_params=pltpu.CompilerParams(
            collective_id=0, has_side_effects=True, vmem_limit_bytes=48 * 1024 * 1024
        ),
    )(
        flow_state, flux_matrices, derivative, penalty, lift_matrices, frequency,
        step_size.reshape(1, LANES), partner,
    )


def solution(mesh):
    placed = (P("inst", None, None, "elem"), P(), P(), P(), P(), P(), P("elem"), P(None, "elem"))
    return jax.shard_map(
        per_device,
        mesh=mesh,
        in_specs=placed,
        out_specs=P("inst", None, None, "elem"),
        check_vma=False,
    )
```

```python
import math

import jax
import jax.numpy as jnp
from jax import lax
from jax.experimental import pallas as pl
from jax.experimental.pallas import tpu as pltpu
from jax.sharding import PartitionSpec as P

MESH = pl.DeviceIdType.MESH
F32 = jnp.float32
BF16 = jnp.bfloat16
HIGHEST = lax.Precision.HIGHEST

STAGES = 4
INST = 4
RING = 8
ROWS = 640
HALF = ROWS // 2
LANES = 128
STREAM = 32
FACE = 25


def split(value):
    high = value.astype(BF16)
    low = (value - high.astype(F32)).astype(BF16)
    return high, low


def kernel(
    flow_ref, flux_hbm, derivative_hbm, penalty_hbm, lift_hbm, frequency_ref, step_hbm, partner_hbm,
    out_ref,
    flux_ref, derivative_ref, penalty_ref, lift_ref, step_ref, partner_ref,
    x_ref, a_send, a_recv, b_send, base_ref, u_ref, ru_ref, wk_ref, wa_ref, wb_ref, wc_ref, ra_ref, rb_ref,
    sh_ref, sl_ref, r_ref, tr_send, tr_recv, t01_ref, zbuf, hbuf, dp_ref, lt_ref, pb_ref, ct_ref, g_ref, lag_ref, seen_ref, mine_ref, tau_ref,
    io_sem, small_sem, as_sem, ar_sem, bs_sem, br_sem, ts_sem, tr_sem, zs_sem, zr_sem, hs_sem, hr_sem, own_sem,
):
    inst = lax.axis_index("inst")
    row = lax.axis_index("elem")
    rows_total = lax.axis_size("elem")
    low = lax.rem(row, RING)
    high = lax.div(row, RING)
    north = lax.rem(row + 1, rows_total)
    south = lax.rem(row + rows_total - 1, rows_total)

    def inst_peer(distance):
        return lax.rem(inst + distance, INST)

    def low_peer(distance):
        return lax.rem(low + distance, RING)

    def high_peer(distance):
        return lax.rem(high + distance, RING)

    @pl.when(inst == 0)
    def _():
        for k in range(STAGES):
            tr_recv[k, 2] = jnp.zeros((2, LANES, LANES), F32)

    @pl.when(inst == INST - 1)
    def _():
        for k in range(STAGES):
            tr_recv[k, 3] = jnp.zeros((2, LANES, LANES), F32)

    barrier = pltpu.get_barrier_semaphore()
    for distance in range(1, INST):
        pl.semaphore_signal(barrier, inc=1, device_id=(inst_peer(distance), row), device_id_type=MESH)
    for other in (north, south):
        pl.semaphore_signal(barrier, inc=1, device_id=(inst, other), device_id_type=MESH)
    for distance in range(1, RING):
        pl.semaphore_signal(
            barrier, inc=1, device_id=(inst, high * RING + low_peer(distance)), device_id_type=MESH
        )
        pl.semaphore_signal(
            barrier, inc=1, device_id=(inst, high_peer(distance) * RING + low), device_id_type=MESH
        )

    loads = [
        pltpu.make_async_copy(
            flow_ref.at[:, :, half, :], x_ref.at[half, :, pl.ds(0, 125), :], io_sem.at[half]
        )
        for half in range(2)
    ]
    small = [
        pltpu.make_async_copy(source, landing, small_sem.at[place])
        for place, (source, landing) in enumerate(
            (
                (derivative_hbm, derivative_ref), (flux_hbm, flux_ref), (penalty_hbm, penalty_ref),
                (lift_hbm, lift_ref), (step_hbm, step_ref), (partner_hbm, partner_ref),
            )
        )
    ]
    for load in loads + small:
        load.start()

    lane = lax.broadcasted_iota(jnp.int32, (1, LANES), 1)

    for load in loads:
        load.wait()
    for half in range(2):
        for var in range(5):
            x_ref[half, var, 125:128, :] = jnp.zeros((3, LANES), F32)
    chunk = 40
    x_rows = x_ref.reshape(2, ROWS, LANES)

    pl.semaphore_wait(barrier, INST - 1 + 2 + 2 * (RING - 1))

    def exchange(send_buffer, recv_buffer, send_sem, recv_sem, distance):
        peer = inst_peer(distance)
        return pltpu.make_async_remote_copy(
            src_ref=send_buffer.at[peer],
            dst_ref=recv_buffer.at[inst],
            send_sem=send_sem.at[peer],
            recv_sem=recv_sem.at[inst],
            device_id=(peer, row),
            device_id_type=MESH,
        )

    def arrival(recv_buffer, send_buffer, send_sem, recv_sem, distance):
        peer = inst_peer(distance)
        return pltpu.make_async_remote_copy(
            src_ref=send_buffer.at[peer],
            dst_ref=recv_buffer.at[peer],
            send_sem=send_sem.at[peer],
            recv_sem=recv_sem.at[peer],
            device_id=(peer, row),
            device_id_type=MESH,
        )

    for distance in (2, 3, 1, 0):
        target = inst_peer(distance)
        turns = [lax.rem(STREAM * quarter + LANES - STREAM * target, LANES) for quarter in range(4)]
        for start in range(0, HALF, chunk):
            packed = None
            for quarter in range(4):
                begin = (quarter // 2) * HALF + start
                moved = pltpu.roll(x_rows[quarter % 2, begin : begin + chunk, :], turns[quarter], 1)
                packed = moved if packed is None else jnp.where(lane >= STREAM * quarter, moved, packed)
            if distance:
                a_send[target, start : start + chunk, :] = packed
            else:
                a_recv[target, start : start + chunk, :] = packed
        if distance:
            exchange(a_send, a_recv, as_sem, ar_sem, distance).start()

    for load in small:
        load.wait()

    dp_ref[...] = jnp.zeros_like(dp_ref)
    for direction in range(3):
        dp_ref[direction, 0:125, 0:125] = derivative_ref[direction]

    def volume(var, carry):
        start = pl.multiple_of(var * 128, 128)
        for other in range(5):
            block = flux_ref[var, 0:1, other : other + 1] * dp_ref[0]
            block = block + flux_ref[var, 1:2, other : other + 1] * dp_ref[1]
            block = block + flux_ref[var, 2:3, other : other + 1] * dp_ref[2]
            fine, rest = split(block)
            wk_ref[pl.ds(start, 128), other * 128 : (other + 1) * 128] = fine
            wk_ref[pl.ds(start, 128), ROWS + other * 128 : ROWS + (other + 1) * 128] = fine
            wk_ref[pl.ds(start, 128), 2 * ROWS + other * 128 : 2 * ROWS + (other + 1) * 128] = rest
        return carry

    lax.fori_loop(0, 5, volume, 0)

    face_column = lax.broadcasted_iota(jnp.int32, (FACE, LANES), 1)
    face_row = lax.broadcasted_iota(jnp.int32, (FACE, LANES), 0)
    repeat = ((lax.rem(face_column, FACE) == face_row) & (face_column < 125)).astype(F32)
    var_column = lax.broadcasted_iota(jnp.int32, (5, LANES), 1)
    var_row = lax.broadcasted_iota(jnp.int32, (5, LANES), 0)
    spread = (lax.div(var_column, FACE) == var_row).astype(F32)
    lt_ref[...] = jnp.zeros_like(lt_ref)
    for face in range(6):
        lt_ref[face, 0:125, :] = lax.dot_general(
            lift_ref[face], repeat, (((0,), (0,)), ((), ())), precision=HIGHEST, preferred_element_type=F32
        )
        pb_ref[face, 0:5, :] = jnp.dot(
            penalty_ref[:, face, :], spread, precision=HIGHEST, preferred_element_type=F32
        )
        target, place, width = (wb_ref, wa_ref, wc_ref)[face // 2], face % 2, 256
        for var in range(5):
            fine, rest = split(lt_ref[face] * pb_ref[face, var : var + 1, :])
            here = slice(var * 128, (var + 1) * 128)
            target[here, place * 128 : (place + 1) * 128] = fine
            target[here, width + place * 128 : width + (place + 1) * 128] = fine
            target[here, 2 * width + place * 128 : 2 * width + (place + 1) * 128] = rest

    g_ref[...] = jnp.zeros_like(g_ref)
    for face in range(2):
        for var in range(5):
            g_ref[face, var * 25 : var * 25 + 25, :] = (
                lt_ref[face, face * 100 : face * 100 + 25, :] * pb_ref[face, var : var + 1, :]
            )
    seen_ref[...] = jnp.zeros_like(seen_ref)
    mine_ref[...] = jnp.zeros_like(mine_ref)
    tau_ref[...] = jnp.zeros_like(tau_ref)

    to_lane = lax.broadcasted_iota(jnp.int32, (256, 256), 1)
    from_lane = lax.broadcasted_iota(jnp.int32, (256, 256), 0)
    apart = to_lane - from_lane
    turns = lax.shift_right_arithmetic(apart, 5) & 7
    aligned = (apart & 31) == 0
    spectral = jnp.zeros((256, 256), F32)
    for turn in range(1, 8):
        if turn != 4:
            weight = 0.5 * (-1) ** turn / math.tan(math.pi * turn / 8)
            spectral = jnp.where(aligned & (turns == turn), weight, spectral)
    spectral = spectral * frequency_ref[0]
    fine, rest = split(spectral)
    sh_ref[...] = fine
    sl_ref[...] = rest

    first = pltpu.roll(step_ref[...], lax.rem((INST - inst) * STREAM, LANES), 1)
    first = jnp.where(lane < STREAM, first, 0.0)
    step_lane = first + pltpu.roll(first, 32, 1) + pltpu.roll(first, 64, 1) + pltpu.roll(first, 96, 1)

    column = jnp.broadcast_to(partner_ref[0:1, :], (8, 8)).astype(F32)
    same = lax.broadcasted_iota(jnp.int32, (8, 8), 0) == lax.broadcasted_iota(jnp.int32, (8, 8), 1)
    column = jnp.sum(jnp.where(same, column, 0.0), axis=1, keepdims=True).astype(jnp.int32)
    ahead = lax.shift_right_arithmetic(jnp.broadcast_to(column, (8, LANES)), 2)
    behind = (2 * row + 128 - ahead) & 63

    t01_ref[...] = jnp.zeros_like(t01_ref)
    ct_ref[...] = jnp.zeros_like(ct_ref)
    tr_send[...] = jnp.zeros_like(tr_send)

    def unpack(side):
        for start in range(0, HALF, chunk):
            even = a_recv[2 * side, start : start + chunk, :]
            odd = a_recv[2 * side + 1, start : start + chunk, :]
            upper = jnp.where(lane < 64, even, pltpu.roll(odd, 64, 1))
            lower = jnp.where(lane < 64, pltpu.roll(even, 64, 1), odd)
            base_ref[side, start : start + chunk, :] = upper
            u_ref[side, start : start + chunk, :] = upper
            base_ref[side, HALF + start : HALF + start + chunk, :] = lower
            u_ref[side, HALF + start : HALF + start + chunk, :] = lower

    near = lax.div(inst, 2)
    for distance in (1, 3):
        @pl.when(lax.rem(inst, 2) == distance // 2)
        def _(distance=distance):
            arrival(a_recv, a_send, as_sem, ar_sem, distance).wait_recv()

    unpack(near)
    arrival(a_recv, a_send, as_sem, ar_sem, 2).wait_recv()
    for distance in (1, 3):
        @pl.when(lax.rem(inst, 2) != distance // 2)
        def _(distance=distance):
            arrival(a_recv, a_send, as_sem, ar_sem, distance).wait_recv()

    unpack(1 - near)

    stream = lane & 31

    def low_copy(k, distance, sender):
        return pltpu.make_async_remote_copy(
            src_ref=zbuf.at[k, sender],
            dst_ref=zbuf.at[k, sender],
            send_sem=zs_sem.at[k],
            recv_sem=zr_sem.at[k],
            device_id=(inst, high * RING + low_peer(distance)),
            device_id_type=MESH,
        )

    def high_copy(k, distance, sender):
        return pltpu.make_async_remote_copy(
            src_ref=hbuf.at[k, sender],
            dst_ref=hbuf.at[k, sender],
            send_sem=hs_sem.at[k],
            recv_sem=hr_sem.at[k],
            device_id=(inst, high_peer(distance) * RING + low),
            device_id_type=MESH,
        )

    def all_of(buffer, k, sem):
        every = buffer.at[k, pl.ds(0, RING - 1)]
        pltpu.make_async_copy(every, every, sem.at[k]).wait()

    def trace_copy(k, sent, landed, device):
        return pltpu.make_async_remote_copy(
            src_ref=tr_send.at[k, sent],
            dst_ref=tr_recv.at[k, landed],
            send_sem=ts_sem.at[k, sent],
            recv_sem=tr_sem.at[k, landed],
            device_id=device,
            device_id_type=MESH,
        )

    def northward(k):
        return trace_copy(k, 1, 0, (inst, north))

    def southward(k):
        return trace_copy(k, 0, 1, (inst, south))

    def upward(k):
        return trace_copy(k, 3, 2, (lax.rem(inst + 1, INST), row))

    def downward(k):
        return trace_copy(k, 2, 3, (lax.rem(inst + INST - 1, INST), row))

    has_above = inst < INST - 1
    has_below = inst > 0

    def interior_traces():
        for side in range(2):
            for var in range(5):
                t01_ref[0, side, var * 25 : var * 25 + 25, :] = u_ref[side, var * 128 : var * 128 + 25, :]
                t01_ref[1, side, var * 25 : var * 25 + 25, :] = u_ref[
                    side, var * 128 + 100 : var * 128 + 125, :
                ]

    own_tau = (step_lane[:, 15:16], step_lane[:, 16:17])

    def slide(k):
        mixed = jnp.where(
            stream == 15,
            t01_ref[1, 0],
            jnp.where(
                stream == 16,
                t01_ref[0, 0],
                jnp.where(stream == 17, pltpu.roll(t01_ref[1, 1], 2, 1), pltpu.roll(t01_ref[0, 1], 2, 1)),
            ),
        )
        ct_ref[0] = jnp.transpose(mixed)
        for kind in range(2):
            slab = jnp.concatenate(
                [ct_ref[0, pl.ds(15 + kind, 4, stride=32), :], ct_ref[0, pl.ds(17 + kind, 4, stride=32), :]], 0
            )
            zbuf[k, low, kind] = jnp.where(lane == 125, own_tau[kind], slab)
        for distance in (4, 3, 5, 2, 6, 1, 7):
            low_copy(k, distance, low).start()

    def section_weight(k):
        return jnp.where(k == 0, 0.25, jnp.where(k == 1, 1.0 / 3.0, jnp.where(k == 2, 0.5, 1.0)))

    interior_traces()
    slide(0)

    def stage(k, carry):
        weight = section_weight(k)

        for side in range(2):
            for var in range(5):
                for depth in range(5):
                    tr_send[k, 0, side, pl.ds(var * 25 + depth, 5, stride=5), :] = u_ref[
                        side, pl.ds(var * 128 + depth, 5, stride=25), :
                    ]
                    tr_send[k, 1, side, pl.ds(var * 25 + depth, 5, stride=5), :] = u_ref[
                        side, pl.ds(var * 128 + 20 + depth, 5, stride=25), :
                    ]
        northward(k).start()
        southward(k).start()
        for side in range(2):
            for var in range(5):
                tr_send[k, 2, side, var * 25 : var * 25 + 25, :] = u_ref[
                    side, pl.ds(var * 128, 25, stride=5), :
                ]
                tr_send[k, 3, side, var * 25 : var * 25 + 25, :] = u_ref[
                    side, pl.ds(var * 128 + 4, 25, stride=5), :
                ]

        @pl.when(has_above)
        def _():
            upward(k).start()

        @pl.when(has_below)
        def _():
            downward(k).start()

        @pl.when(k > 0)
        def _():
            interior_traces()

        last = section_weight(k - 1)
        returned = (
            lax.dot_general(
                jnp.concatenate([seen_ref[1], mine_ref[1]], 0), g_ref[1], (((1,), (1,)), ((), ())),
                precision=HIGHEST, preferred_element_type=F32,
            ),
            lax.dot_general(
                jnp.concatenate([seen_ref[0], mine_ref[0]], 0), g_ref[0], (((1,), (1,)), ((), ())),
                precision=HIGHEST, preferred_element_type=F32,
            ),
        )
        for kind in range(2):
            mine_ref[kind] = zbuf[k, low, kind] - (last * own_tau[kind]) * returned[kind][0:8]
            lag_ref[kind] = (last * tau_ref[kind]) * returned[kind][8:16]

        for side in range(2):
            here = slice(side * LANES, (side + 1) * LANES)
            fine, rest = split(u_ref[side])
            ru_ref[0:ROWS, here] = fine
            ru_ref[ROWS : 2 * ROWS, here] = rest
            ru_ref[2 * ROWS : 3 * ROWS, here] = fine
        r_ref[...] = jnp.dot(wk_ref[...], ru_ref[...], preferred_element_type=F32)
        r_ref[...] += jnp.dot(ru_ref[0:ROWS, :], sh_ref[...], preferred_element_type=F32)
        r_ref[...] += jnp.dot(ru_ref[ROWS : 2 * ROWS, :], sh_ref[...], preferred_element_type=F32)
        r_ref[...] += jnp.dot(ru_ref[0:ROWS, :], sl_ref[...], preferred_element_type=F32)

        for side in range(2):
            here = slice(side * LANES, (side + 1) * LANES)
            west = jnp.where((stream == 0) | (stream == 16), 0.0, pltpu.roll(t01_ref[1, side], 1, 1))
            east = jnp.where((stream == 31) | (stream == 15), 0.0, pltpu.roll(t01_ref[0, side], 127, 1))
            for face, value in ((0, west), (1, east)):
                fine, rest = split(value - t01_ref[face, side])
                rb_ref[face * 128 : (face + 1) * 128, here] = fine
                rb_ref[256 + face * 128 : 256 + (face + 1) * 128, here] = rest
                rb_ref[512 + face * 128 : 512 + (face + 1) * 128, here] = fine
        r_ref[...] += jnp.dot(wb_ref[...], rb_ref[...], preferred_element_type=F32)

        all_of(zbuf, k, zr_sem)
        rotor = zbuf[k, 0, 0]
        stator = zbuf[k, 0, 1]
        for other in range(1, RING):
            rotor = jnp.where((ahead & 7) == other, zbuf[k, other, 0], rotor)
            stator = jnp.where((behind & 7) == other, zbuf[k, other, 1], stator)
        hbuf[k, high, 0] = rotor
        hbuf[k, high, 1] = stator
        for distance in (3, 5, 2, 6, 1, 7, 4):
            high_copy(k, distance, high).start()

        @pl.when(has_below)
        def _():
            upward(k).wait_recv()

        @pl.when(has_above)
        def _():
            downward(k).wait_recv()

        def jumps(faces):
            for place, face in enumerate(faces):
                for side in range(2):
                    here = slice(side * LANES, (side + 1) * LANES)
                    fine, rest = split(tr_recv[k, face, side] - tr_send[k, face, side])
                    ra_ref[place * 128 : (place + 1) * 128, here] = fine
                    ra_ref[256 + place * 128 : 256 + (place + 1) * 128, here] = rest
                    ra_ref[512 + place * 128 : 512 + (place + 1) * 128, here] = fine

        jumps((2, 3))
        r_ref[...] += jnp.dot(wc_ref[...], ra_ref[...], preferred_element_type=F32)

        northward(k).wait_recv()
        southward(k).wait_recv()
        jumps((0, 1))
        r_ref[...] += jnp.dot(wa_ref[...], ra_ref[...], preferred_element_type=F32)

        scale = weight * step_lane
        for side in range(2):
            u_ref[side] = base_ref[side] - scale * r_ref[:, side * LANES : (side + 1) * LANES]

        @pl.when(k < STAGES - 1)
        def _():
            interior_traces()
            slide(k + 1)

        all_of(hbuf, k, hr_sem)
        rotor = hbuf[k, 0, 0]
        stator = hbuf[k, 0, 1]
        for other in range(1, RING):
            rotor = jnp.where(lax.shift_right_arithmetic(ahead, 3) == other, hbuf[k, other, 0], rotor)
            stator = jnp.where(lax.shift_right_arithmetic(behind, 3) == other, hbuf[k, other, 1], stator)

        @pl.when(k == 0)
        def _():
            tau_ref[0] = jnp.broadcast_to(rotor[:, 125:126], (8, LANES))
            tau_ref[1] = jnp.broadcast_to(stator[:, 125:126], (8, LANES))

        rotor = rotor - lag_ref[0]
        stator = stator - lag_ref[1]
        seen_ref[0] = rotor
        seen_ref[1] = stator
        ct_ref[1, pl.ds(16, 4, stride=32), :] = rotor[0:4]
        ct_ref[1, pl.ds(14, 4, stride=32), :] = rotor[4:8]
        ct_ref[1, pl.ds(15, 4, stride=32), :] = stator[0:4]
        ct_ref[1, pl.ds(13, 4, stride=32), :] = stator[4:8]
        across = jnp.transpose(ct_ref[1])
        for side in range(2):
            here = slice(side * LANES, (side + 1) * LANES)
            moved = across if side == 0 else pltpu.roll(across, 2, 1)
            for face, place in ((0, 16), (1, 15)):
                fine, rest = split(jnp.where(stream == place, moved, 0.0))
                rb_ref[face * 128 : (face + 1) * 128, here] = fine
                rb_ref[256 + face * 128 : 256 + (face + 1) * 128, here] = rest
                rb_ref[512 + face * 128 : 512 + (face + 1) * 128, here] = fine
        r_ref[...] = jnp.dot(wb_ref[...], rb_ref[...], preferred_element_type=F32)
        for side in range(2):
            u_ref[side] -= scale * r_ref[:, side * LANES : (side + 1) * LANES]

        northward(k).wait_send()
        southward(k).wait_send()

        @pl.when(has_above)
        def _():
            upward(k).wait_send()

        @pl.when(has_below)
        def _():
            downward(k).wait_send()

        all_of(zbuf, k, zs_sem)
        all_of(hbuf, k, hs_sem)
        return carry

    lax.fori_loop(0, STAGES, stage, 0)

    for distance in (2, 3, 1, 0):
        target = inst_peer(distance)
        side = lax.div(target, 2)
        turn = 64 * lax.rem(target, 2)
        for start in range(0, HALF, chunk):
            upper = pltpu.roll(u_ref[side, start : start + chunk, :], turn, 1)
            lower = pltpu.roll(u_ref[side, HALF + start : HALF + start + chunk, :], 64 - turn, 1)
            packed = jnp.where(lane < 64, upper, lower)
            b_send[target, start : start + chunk, :] = packed
        if distance:
            exchange(b_send, out_ref, bs_sem, br_sem, distance).start()
    own = pltpu.make_async_copy(b_send.at[inst], out_ref.at[inst], own_sem)
    own.start()
    for distance in range(1, INST):
        exchange(a_send, a_recv, as_sem, ar_sem, distance).wait_send()
    for distance in range(1, INST):
        exchange(b_send, out_ref, bs_sem, br_sem, distance).wait_send()
    own.wait()
    for distance in (1, 3, 2):
        arrival(out_ref, b_send, bs_sem, br_sem, distance).wait_recv()


def finish(parts_hbm, out_ref, parts_ref, x_ref, in_sem, out_sem):
    lane = lax.broadcasted_iota(jnp.int32, (1, LANES), 1)
    pieces = 4
    piece = HALF // pieces
    loads = [
        pltpu.make_async_copy(
            parts_hbm.at[:, pl.ds(part * piece, piece), :], parts_ref.at[:, pl.ds(part * piece, piece), :],
            in_sem.at[part],
        )
        for part in range(pieces)
    ]

    def store(var):
        return [
            pltpu.make_async_copy(
                x_ref.at[half, pl.ds(var * 128, 125), :], out_ref.at[var, :, half, :], out_sem.at[half * 5 + var]
            )
            for half in range(2)
        ]

    for load in loads:
        load.start()
    for part in range(pieces):
        loads[part].wait()
        for start in range(part * piece, (part + 1) * piece, 40):
            parts = [parts_ref[source, start : start + 40, :] for source in range(INST)]
            for quarter in range(4):
                whole = None
                for source in range(INST):
                    turn = (STREAM * (source - quarter)) % LANES
                    moved = parts[source] if turn == 0 else pltpu.roll(parts[source], turn, 1)
                    whole = moved if whole is None else jnp.where(lane >= STREAM * source, moved, whole)
                begin = (quarter // 2) * HALF + start
                x_ref[quarter % 2, begin : begin + 40, :] = whole
        for var in ((), (0,), (3,), (1, 2, 4))[part]:
            for copy in store(var):
                copy.start()
    for var in range(5):
        for copy in store(var):
            copy.wait()


def per_device(
    flow_state, flux_matrices, derivative, penalty, lift_matrices, frequency, step_size, partner
):
    outside = pl.BlockSpec(memory_space=pltpu.HBM)
    scalar = pl.BlockSpec(memory_space=pltpu.SMEM)
    dma = pltpu.SemaphoreType.DMA
    parts = pl.pallas_call(
        kernel,
        out_shape=jax.ShapeDtypeStruct((INST, HALF, LANES), F32),
        in_specs=[outside, outside, outside, outside, outside, scalar, outside, outside],
        out_specs=outside,
        scratch_shapes=[
            pltpu.VMEM((5, 3, 5), F32),
            pltpu.VMEM((3, 125, 125), F32),
            pltpu.VMEM((5, 6, 5), F32),
            pltpu.VMEM((6, FACE, 125), F32),
            pltpu.VMEM((1, LANES), F32),
            pltpu.VMEM((4, 8), jnp.int32),
            pltpu.VMEM((2, 5, LANES, LANES), F32),
            pltpu.VMEM((INST, HALF, LANES), F32),
            pltpu.VMEM((INST, HALF, LANES), F32),
            pltpu.VMEM((INST, HALF, LANES), F32),
            pltpu.VMEM((2, ROWS, LANES), F32),
            pltpu.VMEM((2, ROWS, LANES), F32),
            pltpu.VMEM((3 * ROWS, 256), BF16),
            pltpu.VMEM((ROWS, 3 * ROWS), BF16),
            pltpu.VMEM((ROWS, 3 * 256), BF16),
            pltpu.VMEM((ROWS, 3 * 256), BF16),
            pltpu.VMEM((ROWS, 3 * 256), BF16),
            pltpu.VMEM((3 * 256, 256), BF16),
            pltpu.VMEM((3 * 256, 256), BF16),
            pltpu.VMEM((256, 256), BF16),
            pltpu.VMEM((256, 256), BF16),
            pltpu.VMEM((ROWS, 256), F32),
            pltpu.VMEM((STAGES, 4, 2, LANES, LANES), F32),
            pltpu.VMEM((STAGES, 4, 2, LANES, LANES), F32),
            pltpu.VMEM((2, 2, LANES, LANES), F32),
            pltpu.VMEM((STAGES, RING, 2, 8, LANES), F32),
            pltpu.VMEM((STAGES, RING, 2, 8, LANES), F32),
            pltpu.VMEM((3, LANES, LANES), F32),
            pltpu.VMEM((6, LANES, LANES), F32),
            pltpu.VMEM((6, 8, LANES), F32),
            pltpu.VMEM((2, LANES, LANES), F32),
            pltpu.VMEM((2, LANES, LANES), F32),
            pltpu.VMEM((2, 8, LANES), F32),
            pltpu.VMEM((2, 8, LANES), F32),
            pltpu.VMEM((2, 8, LANES), F32),
            pltpu.VMEM((2, 8, LANES), F32),
            dma((2,)),
            dma((6,)),
            dma((INST,)),
            dma((INST,)),
            dma((INST,)),
            dma((INST,)),
            dma((STAGES, 4)),
            dma((STAGES, 4)),
            dma((STAGES,)),
            dma((STAGES,)),
            dma((STAGES,)),
            dma((STAGES,)),
            dma,
        ],
        compiler_params=pltpu.CompilerParams(
            collective_id=0, has_side_effects=True, vmem_limit_bytes=67_043_328
        ),
    )(
        jnp.transpose(flow_state, (1, 2, 0, 3)), jnp.transpose(flux_matrices, (1, 0, 2)), derivative,
        jnp.transpose(penalty, (1, 0, 2)), jnp.transpose(lift_matrices, (0, 2, 1)), frequency,
        step_size.reshape(1, LANES), jnp.transpose(partner, (1, 0)),
    )
    result = pl.pallas_call(
        finish,
        out_shape=jax.ShapeDtypeStruct((5, 125, 2, LANES), F32),
        in_specs=[outside],
        out_specs=outside,
        scratch_shapes=[
            pltpu.VMEM((INST, HALF, LANES), F32),
            pltpu.VMEM((2, ROWS, LANES), F32),
            dma((4,)),
            dma((10,)),
        ],
        compiler_params=pltpu.CompilerParams(vmem_limit_bytes=67_043_328),
    )(parts)
    return jnp.transpose(result, (2, 0, 1, 3))


def solution(mesh):
    placed = (P("inst", None, None, "elem"), P(), P(), P(), P(), P(), P("elem"), P(None, "elem"))
    return jax.shard_map(
        per_device,
        mesh=mesh,
        in_specs=placed,
        out_specs=P("inst", None, None, "elem"),
        check_vma=False,
    )
```

```python
import math

import jax
import jax.numpy as jnp
from jax import lax
from jax.experimental import pallas as pl
from jax.experimental.pallas import tpu as pltpu
from jax.sharding import PartitionSpec as P

MESH = pl.DeviceIdType.MESH
F32 = jnp.float32
BF16 = jnp.bfloat16
HIGHEST = lax.Precision.HIGHEST

STAGES = 4
INST = 4
RING = 8
ROWS = 640
HALF = ROWS // 2
LANES = 128
STREAM = 32
FACE = 25


def split(value):
    high = value.astype(BF16)
    low = (value - high.astype(F32)).astype(BF16)
    return high, low


def halves(left, right):
    middle = left.shape[0] // 2
    return jnp.concatenate(
        [
            jnp.dot(left[:middle, :], right[...], preferred_element_type=F32),
            jnp.dot(left[middle:, :], right[...], preferred_element_type=F32),
        ],
        0,
    )


def kernel(
    flow_ref, flux_hbm, derivative_hbm, penalty_hbm, lift_hbm, frequency_hbm, step_hbm, partner_hbm,
    out_ref,
    flux_ref, derivative_ref, penalty_ref, lift_ref, step_ref, partner_ref, frequency_ref,
    x_ref, a_send, a_recv, b_send, base_ref, u_ref, ru_ref, wk_ref, wa_ref, wb_ref, wc_ref, ra_ref, rb_ref,
    sh_ref, sl_ref, r_ref, tr_send, tr_recv, t01_ref, zbuf, hbuf, dp_ref, lt_ref, pb_ref, ct_ref, g_ref, lag_ref, seen_ref, mine_ref, tau_ref,
    io_sem, small_sem, as_sem, ar_sem, bs_sem, br_sem, ps_sem, us_sem, ds_sem, zs_sem, hs_sem,
    pr_sem, ur_sem, dr_sem, zr_sem, hr_sem, own_sem,
):
    inst = lax.axis_index("inst")
    row = lax.axis_index("elem")
    rows_total = lax.axis_size("elem")
    low = lax.rem(row, RING)
    high = lax.div(row, RING)
    north = lax.rem(row + 1, rows_total)
    south = lax.rem(row + rows_total - 1, rows_total)

    def inst_peer(distance):
        return lax.rem(inst + distance, INST)

    def low_peer(distance):
        return lax.rem(low + distance, RING)

    def high_peer(distance):
        return lax.rem(high + distance, RING)

    @pl.when(inst == 0)
    def _():
        for k in range(STAGES):
            tr_recv[k, :, 2] = jnp.zeros((2, LANES, LANES), F32)

    @pl.when(inst == INST - 1)
    def _():
        for k in range(STAGES):
            tr_recv[k, :, 3] = jnp.zeros((2, LANES, LANES), F32)

    barrier = pltpu.get_barrier_semaphore()
    for distance in range(1, INST):
        pl.semaphore_signal(barrier, inc=1, device_id=(inst_peer(distance), row), device_id_type=MESH)
    for other in (north, south):
        pl.semaphore_signal(barrier, inc=1, device_id=(inst, other), device_id_type=MESH)
    for distance in range(1, RING):
        pl.semaphore_signal(
            barrier, inc=1, device_id=(inst, high * RING + low_peer(distance)), device_id_type=MESH
        )
        pl.semaphore_signal(
            barrier, inc=1, device_id=(inst, high_peer(distance) * RING + low), device_id_type=MESH
        )

    loads = [
        pltpu.make_async_copy(
            flow_ref.at[:, :, half, :], x_ref.at[half, :, pl.ds(0, 125), :], io_sem.at[half]
        )
        for half in range(2)
    ]
    small = [
        pltpu.make_async_copy(source, landing, small_sem.at[place])
        for place, (source, landing) in enumerate(
            (
                (derivative_hbm, derivative_ref), (flux_hbm, flux_ref), (penalty_hbm, penalty_ref),
                (lift_hbm, lift_ref), (step_hbm, step_ref), (partner_hbm, partner_ref),
                (frequency_hbm, frequency_ref),
            )
        )
    ]
    for load in loads + small:
        load.start()

    lane = lax.broadcasted_iota(jnp.int32, (1, LANES), 1)

    for load in loads:
        load.wait()
    for half in range(2):
        for var in range(5):
            x_ref[half, var, 125:128, :] = jnp.zeros((3, LANES), F32)
    chunk = 40
    x_rows = x_ref.reshape(2, ROWS, LANES)

    pl.semaphore_wait(barrier, INST - 1 + 2 + 2 * (RING - 1))

    partner_inst = inst + 1 - 2 * lax.rem(inst, 2)
    peers = (inst_peer(2), INST - 1 - inst, partner_inst, inst)

    def exchange(send_buffer, recv_buffer, send_sem, recv_sem, peer):
        return pltpu.make_async_remote_copy(
            src_ref=send_buffer.at[peer],
            dst_ref=recv_buffer.at[inst],
            send_sem=send_sem,
            recv_sem=recv_sem.at[inst],
            device_id=(peer, row),
            device_id_type=MESH,
        )

    def arrival(recv_buffer, send_buffer, send_sem, recv_sem, peer):
        return pltpu.make_async_remote_copy(
            src_ref=send_buffer.at[peer],
            dst_ref=recv_buffer.at[peer],
            send_sem=send_sem,
            recv_sem=recv_sem.at[peer],
            device_id=(peer, row),
            device_id_type=MESH,
        )

    for order, target in enumerate(peers):
        remote = order < INST - 1
        turns = [lax.rem(STREAM * quarter + LANES - STREAM * target, LANES) for quarter in range(4)]
        for start in range(0, HALF, chunk):
            packed = None
            for quarter in range(4):
                begin = (quarter // 2) * HALF + start
                moved = pltpu.roll(x_rows[quarter % 2, begin : begin + chunk, :], turns[quarter], 1)
                packed = moved if packed is None else jnp.where(lane >= STREAM * quarter, moved, packed)
            if remote:
                a_send[target, start : start + chunk, :] = packed
            else:
                a_recv[target, start : start + chunk, :] = packed
        if remote:
            exchange(a_send, a_recv, as_sem, ar_sem, target).start()

    for load in small:
        load.wait()

    dp_ref[...] = jnp.zeros_like(dp_ref)
    for direction in range(3):
        dp_ref[direction, 0:125, 0:125] = derivative_ref[direction]

    def volume(var, carry):
        start = pl.multiple_of(var * 128, 128)
        for other in range(5):
            block = flux_ref[var, 0:1, other : other + 1] * dp_ref[0]
            block = block + flux_ref[var, 1:2, other : other + 1] * dp_ref[1]
            block = block + flux_ref[var, 2:3, other : other + 1] * dp_ref[2]
            fine, rest = split(block)
            wk_ref[pl.ds(start, 128), other * 128 : (other + 1) * 128] = fine
            wk_ref[pl.ds(start, 128), ROWS + other * 128 : ROWS + (other + 1) * 128] = fine
            wk_ref[pl.ds(start, 128), 2 * ROWS + other * 128 : 2 * ROWS + (other + 1) * 128] = rest
        return carry

    lax.fori_loop(0, 5, volume, 0)

    face_column = lax.broadcasted_iota(jnp.int32, (FACE, LANES), 1)
    face_row = lax.broadcasted_iota(jnp.int32, (FACE, LANES), 0)
    repeat = ((lax.rem(face_column, FACE) == face_row) & (face_column < 125)).astype(F32)
    var_column = lax.broadcasted_iota(jnp.int32, (5, LANES), 1)
    var_row = lax.broadcasted_iota(jnp.int32, (5, LANES), 0)
    spread = (lax.div(var_column, FACE) == var_row).astype(F32)
    lt_ref[...] = jnp.zeros_like(lt_ref)
    for face in range(6):
        lt_ref[face, 0:125, :] = lax.dot_general(
            lift_ref[face], repeat, (((0,), (0,)), ((), ())), precision=HIGHEST, preferred_element_type=F32
        )
        pb_ref[face, 0:5, :] = jnp.dot(
            penalty_ref[:, face, :], spread, precision=HIGHEST, preferred_element_type=F32
        )
        target, place, width = (wb_ref, wa_ref, wc_ref)[face // 2], face % 2, 256
        for var in range(5):
            fine, rest = split(lt_ref[face] * pb_ref[face, var : var + 1, :])
            here = slice(var * 128, (var + 1) * 128)
            target[here, place * 128 : (place + 1) * 128] = fine
            target[here, width + place * 128 : width + (place + 1) * 128] = fine
            target[here, 2 * width + place * 128 : 2 * width + (place + 1) * 128] = rest

    g_ref[...] = jnp.zeros_like(g_ref)
    for face in range(2):
        for var in range(5):
            g_ref[face, var * 25 : var * 25 + 25, :] = (
                lt_ref[face, face * 100 : face * 100 + 25, :] * pb_ref[face, var : var + 1, :]
            )
    seen_ref[...] = jnp.zeros_like(seen_ref)
    mine_ref[...] = jnp.zeros_like(mine_ref)
    tau_ref[...] = jnp.zeros_like(tau_ref)

    to_lane = lax.broadcasted_iota(jnp.int32, (256, 256), 1)
    from_lane = lax.broadcasted_iota(jnp.int32, (256, 256), 0)
    apart = to_lane - from_lane
    turns = lax.shift_right_arithmetic(apart, 5) & 7
    aligned = (apart & 31) == 0
    spectral = jnp.zeros((256, 256), F32)
    for turn in range(1, 8):
        if turn != 4:
            weight = 0.5 * (-1) ** turn / math.tan(math.pi * turn / 8)
            spectral = jnp.where(aligned & (turns == turn), weight, spectral)
    spectral = spectral * frequency_ref[...]
    fine, rest = split(spectral)
    sh_ref[...] = fine
    sl_ref[...] = rest

    first = pltpu.roll(step_ref[...], lax.rem((INST - inst) * STREAM, LANES), 1)
    first = jnp.where(lane < STREAM, first, 0.0)
    step_lane = first + pltpu.roll(first, 32, 1) + pltpu.roll(first, 64, 1) + pltpu.roll(first, 96, 1)

    column = jnp.broadcast_to(partner_ref[0:1, :], (8, 8)).astype(F32)
    same = lax.broadcasted_iota(jnp.int32, (8, 8), 0) == lax.broadcasted_iota(jnp.int32, (8, 8), 1)
    column = jnp.sum(jnp.where(same, column, 0.0), axis=1, keepdims=True).astype(jnp.int32)
    ahead = lax.shift_right_arithmetic(jnp.broadcast_to(column, (8, LANES)), 2)
    behind = (2 * row + 128 - ahead) & 63

    wanted = tuple(
        jnp.concatenate([ahead[4 * side : 4 * side + 4], behind[4 * side : 4 * side + 4]], 0) for side in range(2)
    )

    t01_ref[...] = jnp.zeros_like(t01_ref)
    ct_ref[...] = jnp.zeros_like(ct_ref)
    tr_send[...] = jnp.zeros_like(tr_send)

    def unpack(side):
        for start in range(0, HALF, chunk):
            even = a_recv[2 * side, start : start + chunk, :]
            odd = a_recv[2 * side + 1, start : start + chunk, :]
            upper = jnp.where(lane < 64, even, pltpu.roll(odd, 64, 1))
            lower = jnp.where(lane < 64, pltpu.roll(even, 64, 1), odd)
            base_ref[side, start : start + chunk, :] = upper
            u_ref[side, start : start + chunk, :] = upper
            base_ref[side, HALF + start : HALF + start + chunk, :] = lower
            u_ref[side, HALF + start : HALF + start + chunk, :] = lower

    stream = lane & 31
    eighth = lax.broadcasted_iota(jnp.int32, (8, LANES), 0)
    own_tau = jnp.where(eighth < 4, step_lane[:, 15:16], step_lane[:, 16:17])
    near = lax.div(inst, 2)
    far = 1 - near

    def hop(buffer, k, side, sender, send_sem, recv_sem, device):
        return pltpu.make_async_remote_copy(
            src_ref=buffer.at[k, side, sender],
            dst_ref=buffer.at[k, side, sender],
            send_sem=send_sem,
            recv_sem=recv_sem.at[k, side],
            device_id=(inst, device),
            device_id_type=MESH,
        )

    def all_of(part, sem):
        pltpu.make_async_copy(part, part, sem).wait()

    def trace_copy(k, side, sent, landed, send_sem, recv_sem, device):
        return pltpu.make_async_remote_copy(
            src_ref=tr_send.at[k, side, sent],
            dst_ref=tr_recv.at[k, side, landed],
            send_sem=send_sem,
            recv_sem=recv_sem.at[k, side],
            device_id=device,
            device_id_type=MESH,
        )

    def upward(k, side):
        return trace_copy(k, side, 3, 2, us_sem, ur_sem, (lax.rem(inst + 1, INST), row))

    def downward(k, side):
        return trace_copy(k, side, 2, 3, ds_sem, dr_sem, (lax.rem(inst + INST - 1, INST), row))

    has_above = inst < INST - 1
    has_below = inst > 0

    def interior_traces(side):
        for var in range(5):
            t01_ref[0, side, var * 25 : var * 25 + 25, :] = u_ref[side, var * 128 : var * 128 + 25, :]
            t01_ref[1, side, var * 25 : var * 25 + 25, :] = u_ref[side, var * 128 + 100 : var * 128 + 125, :]

    def slide(k, side):
        ct_ref[0] = jnp.transpose(jnp.where(stream == 15, t01_ref[1, side], t01_ref[0, side]))
        slab = jnp.concatenate([ct_ref[0, pl.ds(15 + kind, 4, stride=32), :] for kind in range(2)], 0)
        zbuf[k, side, low] = jnp.where(lane == 125, own_tau, slab)
        for distance in (4, 3, 5, 2, 6, 1, 7):
            hop(zbuf, k, side, low, zs_sem, zr_sem, high * RING + low_peer(distance)).start()

    def send_traces(k, side):
        for var in range(5):
            for depth in range(5):
                for face in range(2):
                    tr_send[k, side, face, pl.ds(var * 25 + depth, 5, stride=5), :] = u_ref[
                        side, pl.ds(var * 128 + 20 * face + depth, 5, stride=25), :
                    ]
        trace_copy(k, side, 1, 0, ps_sem, pr_sem, (inst, north)).start()
        trace_copy(k, side, 0, 1, ps_sem, pr_sem, (inst, south)).start()
        for var in range(5):
            for face in range(2):
                tr_send[k, side, 2 + face, var * 25 : var * 25 + 25, :] = u_ref[
                    side, pl.ds(var * 128 + 4 * face, 25, stride=5), :
                ]

        @pl.when(has_above)
        def _():
            upward(k, side).start()

        @pl.when(has_below)
        def _():
            downward(k, side).start()

    def begin(side):
        unpack(side)
        interior_traces(side)
        slide(0, side)
        send_traces(0, side)

    arrival(a_recv, a_send, as_sem, ar_sem, partner_inst).wait_recv()
    begin(near)
    for peer in peers[:2]:
        arrival(a_recv, a_send, as_sem, ar_sem, peer).wait_recv()
    begin(far)

    def section_weight(k):
        return jnp.where(k == 0, 0.25, jnp.where(k == 1, 1.0 / 3.0, jnp.where(k == 2, 0.5, 1.0)))

    def pick(buffer, k, side, digit):
        wanted_here = jnp.where(side == 0, wanted[0], wanted[1])
        digits = wanted_here & 7 if digit == 0 else lax.shift_right_arithmetic(wanted_here, 3)
        picked = buffer[k, side, 0]
        for other in range(1, RING):
            picked = jnp.where(digits == other, buffer[k, side, other], picked)
        return picked

    def place(target, start, value):
        fine, rest = split(value)
        target[start : start + 128, :] = fine
        target[256 + start : 256 + start + 128, :] = rest
        target[512 + start : 512 + start + 128, :] = fine

    def stage(k, carry):
        weight = section_weight(k)
        last = section_weight(k - 1)
        scale = weight * step_lane

        @pl.when(k > 0)
        def _():
            interior_traces(0)
            interior_traces(1)

        known = jnp.concatenate([seen_ref[0], mine_ref[0], seen_ref[1], mine_ref[1]], 0)
        through = [
            lax.dot_general(
                known, g_ref[face], (((1,), (1,)), ((), ())), precision=HIGHEST, preferred_element_type=F32
            )
            for face in range(2)
        ]
        for side in range(2):
            back = [
                jnp.concatenate([through[1][start + 4 : start + 8], through[0][start : start + 4]], 0)
                for start in (16 * side, 16 * side + 8)
            ]
            mine_ref[side] = zbuf[k, side, low] - (last * own_tau) * back[0]
            lag_ref[side] = (last * tau_ref[side]) * back[1]

        for side in range(2):
            here = slice(side * LANES, (side + 1) * LANES)
            fine, rest = split(u_ref[side])
            ru_ref[0:ROWS, here] = fine
            ru_ref[ROWS : 2 * ROWS, here] = rest
            ru_ref[2 * ROWS : 3 * ROWS, here] = fine
            west = jnp.where((stream == 0) | (stream == 16), 0.0, pltpu.roll(t01_ref[1, side], 1, 1))
            east = jnp.where((stream == 31) | (stream == 15), 0.0, pltpu.roll(t01_ref[0, side], 127, 1))
            for face, value in ((0, west), (1, east)):
                fine, rest = split(value - t01_ref[face, side])
                rb_ref[face * 128 : (face + 1) * 128, here] = fine
                rb_ref[256 + face * 128 : 256 + (face + 1) * 128, here] = rest
                rb_ref[512 + face * 128 : 512 + (face + 1) * 128, here] = fine

        def add(left, right, first=False):
            both = halves(left, right)
            for side in range(2):
                part = both[:, side * LANES : (side + 1) * LANES]
                if first:
                    r_ref[side] = part
                else:
                    r_ref[side] += part

        add(wk_ref, ru_ref, True)
        add(ru_ref.at[0:ROWS], sh_ref)
        add(ru_ref.at[ROWS : 2 * ROWS], sh_ref)
        add(ru_ref.at[0:ROWS], sl_ref)
        add(wb_ref, rb_ref)

        for side in (near, far):
            all_of(zbuf.at[k, side, pl.ds(0, RING - 1)], zr_sem.at[k, side])
            hbuf[k, side, high] = pick(zbuf, k, side, 0)
            for distance in (3, 5, 2, 6, 1, 7, 4):
                hop(hbuf, k, side, high, hs_sem, hr_sem, high_peer(distance) * RING + low).start()

        for side in (near, far):
            @pl.when(has_below)
            def _(side=side):
                upward(k, side).wait_recv()

            @pl.when(has_above)
            def _(side=side):
                downward(k, side).wait_recv()

            for face in range(2):
                place(ra_ref, face * 128, tr_recv[k, side, 2 + face] - tr_send[k, side, 2 + face])
            r_ref[side] += halves(wc_ref, ra_ref)
            all_of(tr_recv.at[k, side, pl.ds(0, 2)], pr_sem.at[k, side])
            for face in range(2):
                place(ra_ref, face * 128, tr_recv[k, side, face] - tr_send[k, side, face])
            total = r_ref[side] + halves(wa_ref, ra_ref)
            u_ref[side] = base_ref[side] - scale * total

            @pl.when(k < STAGES - 1)
            def _(side=side):
                interior_traces(side)
                slide(k + 1, side)

        for side in (near, far):
            all_of(hbuf.at[k, side, pl.ds(0, RING - 1)], hr_sem.at[k, side])
            seen = pick(hbuf, k, side, 1)

            @pl.when(k == 0)
            def _(side=side, seen=seen):
                tau_ref[side] = jnp.broadcast_to(seen[:, 125:126], (8, LANES))

            seen = seen - lag_ref[side]
            seen_ref[side] = seen
            ct_ref[1, pl.ds(16, 4, stride=32), :] = seen[0:4]
            ct_ref[1, pl.ds(15, 4, stride=32), :] = seen[4:8]
            across = jnp.transpose(ct_ref[1])
            for face in range(2):
                place(ra_ref, face * 128, jnp.where(stream == 16 - face, across, 0.0))
            u_ref[side] -= scale * halves(wb_ref, ra_ref)

            @pl.when(k < STAGES - 1)
            def _(side=side):
                send_traces(k + 1, side)
        return carry

    lax.fori_loop(0, STAGES, stage, 0)

    for order, target in enumerate(peers):
        side = lax.div(target, 2)
        turn = 64 * lax.rem(target, 2)
        for start in range(0, HALF, chunk):
            upper = pltpu.roll(u_ref[side, start : start + chunk, :], turn, 1)
            lower = pltpu.roll(u_ref[side, HALF + start : HALF + start + chunk, :], 64 - turn, 1)
            packed = jnp.where(lane < 64, upper, lower)
            b_send[target, start : start + chunk, :] = packed
        if order < INST - 1:
            exchange(b_send, out_ref, bs_sem, br_sem, target).start()
    own = pltpu.make_async_copy(b_send.at[inst], out_ref.at[inst], own_sem)
    own.start()
    all_of(a_send.at[pl.ds(0, INST - 1)], as_sem)
    all_of(b_send.at[pl.ds(0, INST - 1)], bs_sem)
    all_of(zbuf.at[:, :, pl.ds(0, RING - 1)], zs_sem)
    all_of(hbuf.at[:, :, pl.ds(0, RING - 1)], hs_sem)
    all_of(tr_send.at[:, :, pl.ds(0, 2)], ps_sem)

    @pl.when(has_above)
    def _():
        all_of(tr_send.at[:, :, 3], us_sem)

    @pl.when(has_below)
    def _():
        all_of(tr_send.at[:, :, 2], ds_sem)

    own.wait()
    for peer in peers[:3]:
        arrival(out_ref, b_send, bs_sem, br_sem, peer).wait_recv()


def finish(parts_hbm, out_ref, parts_ref, x_ref, in_sem, out_sem):
    lane = lax.broadcasted_iota(jnp.int32, (1, LANES), 1)
    pieces = 4
    piece = HALF // pieces
    loads = [
        pltpu.make_async_copy(
            parts_hbm.at[:, pl.ds(part * piece, piece), :], parts_ref.at[:, pl.ds(part * piece, piece), :],
            in_sem.at[part],
        )
        for part in range(pieces)
    ]

    def runs(part):
        found = []
        for upper in range(2):
            first, end = upper * HALF + part * piece, upper * HALF + (part + 1) * piece
            while first < end:
                var, node = divmod(first, 128)
                stop = min(end, (var + 1) * 128)
                found.append((var, node, min(stop, var * 128 + 125) - first))
                first = stop
        return found

    for load in loads:
        load.start()
    for part in range(pieces):
        loads[part].wait()
        for start in range(part * piece, (part + 1) * piece, 40):
            parts = [parts_ref[source, start : start + 40, :] for source in range(INST)]
            for quarter in range(4):
                whole = None
                for source in range(INST):
                    turn = (STREAM * (source - quarter)) % LANES
                    moved = parts[source] if turn == 0 else pltpu.roll(parts[source], turn, 1)
                    whole = moved if whole is None else jnp.where(lane >= STREAM * source, moved, whole)
                begin = (quarter // 2) * HALF + start
                x_ref[quarter % 2, begin : begin + 40, :] = whole
        for var, node, count in runs(part):
            for half in range(2):
                pltpu.make_async_copy(
                    x_ref.at[half, pl.ds(var * 128 + node, count), :],
                    out_ref.at[var, pl.ds(node, count), half, :],
                    out_sem.at[part],
                ).start()
    for part in range(pieces):
        every = x_ref.at[0, pl.ds(0, 2 * sum(count for _, _, count in runs(part))), :]
        pltpu.make_async_copy(every, every, out_sem.at[part]).wait()


def per_device(
    flow_state, flux_matrices, derivative, penalty, lift_matrices, frequency, step_size, partner
):
    outside = pl.BlockSpec(memory_space=pltpu.HBM)
    dma = pltpu.SemaphoreType.DMA
    parts = pl.pallas_call(
        kernel,
        out_shape=jax.ShapeDtypeStruct((INST, HALF, LANES), F32),
        in_specs=[outside, outside, outside, outside, outside, outside, outside, outside],
        out_specs=outside,
        scratch_shapes=[
            pltpu.VMEM((5, 3, 5), F32),
            pltpu.VMEM((3, 125, 125), F32),
            pltpu.VMEM((5, 6, 5), F32),
            pltpu.VMEM((6, FACE, 125), F32),
            pltpu.VMEM((1, LANES), F32),
            pltpu.VMEM((4, 8), jnp.int32),
            pltpu.VMEM((1, 1), F32),
            pltpu.VMEM((2, 5, LANES, LANES), F32),
            pltpu.VMEM((INST, HALF, LANES), F32),
            pltpu.VMEM((INST, HALF, LANES), F32),
            pltpu.VMEM((INST, HALF, LANES), F32),
            pltpu.VMEM((2, ROWS, LANES), F32),
            pltpu.VMEM((2, ROWS, LANES), F32),
            pltpu.VMEM((3 * ROWS, 256), BF16),
            pltpu.VMEM((ROWS, 3 * ROWS), BF16),
            pltpu.VMEM((ROWS, 3 * 256), BF16),
            pltpu.VMEM((ROWS, 3 * 256), BF16),
            pltpu.VMEM((ROWS, 3 * 256), BF16),
            pltpu.VMEM((3 * 256, LANES), BF16),
            pltpu.VMEM((3 * 256, 256), BF16),
            pltpu.VMEM((256, 256), BF16),
            pltpu.VMEM((256, 256), BF16),
            pltpu.VMEM((2, ROWS, LANES), F32),
            pltpu.VMEM((STAGES, 2, 4, LANES, LANES), F32),
            pltpu.VMEM((STAGES, 2, 4, LANES, LANES), F32),
            pltpu.VMEM((2, 2, LANES, LANES), F32),
            pltpu.VMEM((STAGES, 2, RING, 8, LANES), F32),
            pltpu.VMEM((STAGES, 2, RING, 8, LANES), F32),
            pltpu.VMEM((3, LANES, LANES), F32),
            pltpu.VMEM((6, LANES, LANES), F32),
            pltpu.VMEM((6, 8, LANES), F32),
            pltpu.VMEM((2, LANES, LANES), F32),
            pltpu.VMEM((2, LANES, LANES), F32),
            pltpu.VMEM((2, 8, LANES), F32),
            pltpu.VMEM((2, 8, LANES), F32),
            pltpu.VMEM((2, 8, LANES), F32),
            pltpu.VMEM((2, 8, LANES), F32),
            dma((2,)),
            dma((7,)),
            dma,
            dma((INST,)),
            dma,
            dma((INST,)),
            dma,
            dma,
            dma,
            dma,
            dma,
            dma((STAGES, 2)),
            dma((STAGES, 2)),
            dma((STAGES, 2)),
            dma((STAGES, 2)),
            dma((STAGES, 2)),
            dma,
        ],
        compiler_params=pltpu.CompilerParams(
            collective_id=0, has_side_effects=True, vmem_limit_bytes=67_043_328
        ),
    )(
        jnp.transpose(flow_state, (1, 2, 0, 3)), jnp.transpose(flux_matrices, (1, 0, 2)), derivative,
        jnp.transpose(penalty, (1, 0, 2)), jnp.transpose(lift_matrices, (0, 2, 1)),
        frequency.reshape(1, 1),
        step_size.reshape(1, LANES), jnp.transpose(partner, (1, 0)),
    )
    result = pl.pallas_call(
        finish,
        out_shape=jax.ShapeDtypeStruct((5, 125, 2, LANES), F32),
        in_specs=[outside],
        out_specs=outside,
        scratch_shapes=[
            pltpu.VMEM((INST, HALF, LANES), F32),
            pltpu.VMEM((2, ROWS, LANES), F32),
            dma((4,)),
            dma((4,)),
        ],
        compiler_params=pltpu.CompilerParams(vmem_limit_bytes=67_043_328),
    )(parts)
    return jnp.transpose(result, (2, 0, 1, 3))


def solution(mesh):
    placed = (P("inst", None, None, "elem"), P(), P(), P(), P(), P(), P("elem"), P(None, "elem"))
    return jax.shard_map(
        per_device,
        mesh=mesh,
        in_specs=placed,
        out_specs=P("inst", None, None, "elem"),
        check_vma=False,
    )
```

```python
import math

import jax
import jax.numpy as jnp
from jax import lax
from jax.experimental import pallas as pl
from jax.experimental.pallas import tpu as pltpu
from jax.sharding import PartitionSpec as P

MESH = pl.DeviceIdType.MESH
F32 = jnp.float32
BF16 = jnp.bfloat16
HIGHEST = lax.Precision.HIGHEST

STAGES = 4
INST = 4
RING = 8
ROWS = 640
HALF = ROWS // 2
LANES = 128
STREAM = 32
FACE = 25


def split(value):
    high = value.astype(BF16)
    low = (value - high.astype(F32)).astype(BF16)
    return high, low


def halves(left, right):
    middle = left.shape[0] // 2
    return jnp.concatenate(
        [
            jnp.dot(left[:middle, :], right[...], preferred_element_type=F32),
            jnp.dot(left[middle:, :], right[...], preferred_element_type=F32),
        ],
        0,
    )


def kernel(
    flow_ref, flux_hbm, derivative_hbm, penalty_hbm, lift_hbm, frequency_hbm, step_hbm, partner_hbm,
    out_ref,
    flux_ref, derivative_ref, penalty_ref, lift_ref, step_ref, partner_ref, frequency_ref,
    x_ref, a_send, a_recv, b_send, base_ref, u_ref, ru_ref, wk_ref, wa_ref, wb_ref, wc_ref, ra_ref, rb_ref,
    sh_ref, sl_ref, r_ref, tr_send, tr_recv, t01_ref, zbuf, hbuf, dp_ref, lt_ref, pb_ref, ct_ref, g_ref, lag_ref, seen_ref, mine_ref, tau_ref,
    io_sem, small_sem, as_sem, ar_sem, bs_sem, br_sem, ps_sem, us_sem, ds_sem, zs_sem, hs_sem,
    pr_sem, ur_sem, dr_sem, zr_sem, hr_sem, own_sem,
):
    inst = lax.axis_index("inst")
    row = lax.axis_index("elem")
    rows_total = lax.axis_size("elem")
    low = lax.rem(row, RING)
    high = lax.div(row, RING)
    north = lax.rem(row + 1, rows_total)
    south = lax.rem(row + rows_total - 1, rows_total)

    def inst_peer(distance):
        return lax.rem(inst + distance, INST)

    def low_peer(distance):
        return lax.rem(low + distance, RING)

    def high_peer(distance):
        return lax.rem(high + distance, RING)

    @pl.when(inst == 0)
    def _():
        for k in range(STAGES):
            tr_recv[k, :, 2] = jnp.zeros((2, LANES, LANES), F32)

    @pl.when(inst == INST - 1)
    def _():
        for k in range(STAGES):
            tr_recv[k, :, 3] = jnp.zeros((2, LANES, LANES), F32)

    barrier = pltpu.get_barrier_semaphore()
    for distance in range(1, INST):
        pl.semaphore_signal(barrier, inc=1, device_id=(inst_peer(distance), row), device_id_type=MESH)
    for other in (north, south):
        pl.semaphore_signal(barrier, inc=1, device_id=(inst, other), device_id_type=MESH)
    for distance in range(1, RING):
        pl.semaphore_signal(
            barrier, inc=1, device_id=(inst, high * RING + low_peer(distance)), device_id_type=MESH
        )
        pl.semaphore_signal(
            barrier, inc=1, device_id=(inst, high_peer(distance) * RING + low), device_id_type=MESH
        )

    loads = [
        pltpu.make_async_copy(
            flow_ref.at[:, :, half, :], x_ref.at[half, :, pl.ds(0, 125), :], io_sem.at[half]
        )
        for half in range(2)
    ]
    small = [
        pltpu.make_async_copy(source, landing, small_sem.at[place])
        for place, (source, landing) in enumerate(
            (
                (derivative_hbm, derivative_ref), (flux_hbm, flux_ref), (penalty_hbm, penalty_ref),
                (lift_hbm, lift_ref), (step_hbm, step_ref), (partner_hbm, partner_ref),
                (frequency_hbm, frequency_ref),
            )
        )
    ]
    for load in loads + small:
        load.start()

    lane = lax.broadcasted_iota(jnp.int32, (1, LANES), 1)

    for load in loads:
        load.wait()
    for half in range(2):
        for var in range(5):
            x_ref[half, var, 125:128, :] = jnp.zeros((3, LANES), F32)
    chunk = 40
    x_rows = x_ref.reshape(2, ROWS, LANES)

    pl.semaphore_wait(barrier, INST - 1 + 2 + 2 * (RING - 1))

    partner_inst = inst + 1 - 2 * lax.rem(inst, 2)
    peers = (inst_peer(2), INST - 1 - inst, partner_inst, inst)

    def exchange(send_buffer, recv_buffer, send_sem, recv_sem, peer):
        return pltpu.make_async_remote_copy(
            src_ref=send_buffer.at[peer],
            dst_ref=recv_buffer.at[inst],
            send_sem=send_sem,
            recv_sem=recv_sem.at[inst],
            device_id=(peer, row),
            device_id_type=MESH,
        )

    def arrival(recv_buffer, send_buffer, send_sem, recv_sem, peer):
        return pltpu.make_async_remote_copy(
            src_ref=send_buffer.at[peer],
            dst_ref=recv_buffer.at[peer],
            send_sem=send_sem,
            recv_sem=recv_sem.at[peer],
            device_id=(peer, row),
            device_id_type=MESH,
        )

    for order, target in enumerate(peers):
        remote = order < INST - 1
        turns = [lax.rem(STREAM * quarter + LANES - STREAM * target, LANES) for quarter in range(4)]
        for start in range(0, HALF, chunk):
            packed = None
            for quarter in range(4):
                begin = (quarter // 2) * HALF + start
                moved = pltpu.roll(x_rows[quarter % 2, begin : begin + chunk, :], turns[quarter], 1)
                packed = moved if packed is None else jnp.where(lane >= STREAM * quarter, moved, packed)
            if remote:
                a_send[target, start : start + chunk, :] = packed
            else:
                a_recv[target, start : start + chunk, :] = packed
        if remote:
            exchange(a_send, a_recv, as_sem, ar_sem, target).start()

    for load in small:
        load.wait()

    dp_ref[...] = jnp.zeros_like(dp_ref)
    for direction in range(3):
        dp_ref[direction, 0:125, 0:125] = derivative_ref[direction]

    def volume(var, carry):
        start = pl.multiple_of(var * 128, 128)
        for other in range(5):
            block = flux_ref[var, 0:1, other : other + 1] * dp_ref[0]
            block = block + flux_ref[var, 1:2, other : other + 1] * dp_ref[1]
            block = block + flux_ref[var, 2:3, other : other + 1] * dp_ref[2]
            fine, rest = split(block)
            wk_ref[pl.ds(start, 128), other * 128 : (other + 1) * 128] = fine
            wk_ref[pl.ds(start, 128), ROWS + other * 128 : ROWS + (other + 1) * 128] = fine
            wk_ref[pl.ds(start, 128), 2 * ROWS + other * 128 : 2 * ROWS + (other + 1) * 128] = rest
        return carry

    lax.fori_loop(0, 5, volume, 0)

    face_column = lax.broadcasted_iota(jnp.int32, (FACE, LANES), 1)
    face_row = lax.broadcasted_iota(jnp.int32, (FACE, LANES), 0)
    repeat = ((lax.rem(face_column, FACE) == face_row) & (face_column < 125)).astype(F32)
    var_column = lax.broadcasted_iota(jnp.int32, (5, LANES), 1)
    var_row = lax.broadcasted_iota(jnp.int32, (5, LANES), 0)
    spread = (lax.div(var_column, FACE) == var_row).astype(F32)
    lt_ref[...] = jnp.zeros_like(lt_ref)
    for face in range(6):
        lt_ref[face, 0:125, :] = lax.dot_general(
            lift_ref[face], repeat, (((0,), (0,)), ((), ())), precision=HIGHEST, preferred_element_type=F32
        )
        pb_ref[face, 0:5, :] = jnp.dot(
            penalty_ref[:, face, :], spread, precision=HIGHEST, preferred_element_type=F32
        )
        target, place, width = (wb_ref, wa_ref, wc_ref)[face // 2], face % 2, 256
        for var in range(5):
            fine, rest = split(lt_ref[face] * pb_ref[face, var : var + 1, :])
            here = slice(var * 128, (var + 1) * 128)
            target[here, place * 128 : (place + 1) * 128] = fine
            target[here, width + place * 128 : width + (place + 1) * 128] = fine
            target[here, 2 * width + place * 128 : 2 * width + (place + 1) * 128] = rest

    g_ref[...] = jnp.zeros_like(g_ref)
    for face in range(2):
        for var in range(5):
            g_ref[face, var * 25 : var * 25 + 25, :] = (
                lt_ref[face, face * 100 : face * 100 + 25, :] * pb_ref[face, var : var + 1, :]
            )
    seen_ref[...] = jnp.zeros_like(seen_ref)
    mine_ref[...] = jnp.zeros_like(mine_ref)
    tau_ref[...] = jnp.zeros_like(tau_ref)

    to_lane = lax.broadcasted_iota(jnp.int32, (256, 256), 1)
    from_lane = lax.broadcasted_iota(jnp.int32, (256, 256), 0)
    apart = to_lane - from_lane
    turns = lax.shift_right_arithmetic(apart, 5) & 7
    aligned = (apart & 31) == 0
    spectral = jnp.zeros((256, 256), F32)
    for turn in range(1, 8):
        if turn != 4:
            weight = 0.5 * (-1) ** turn / math.tan(math.pi * turn / 8)
            spectral = jnp.where(aligned & (turns == turn), weight, spectral)
    spectral = spectral * frequency_ref[...]
    fine, rest = split(spectral)
    sh_ref[...] = fine
    sl_ref[...] = rest

    first = pltpu.roll(step_ref[...], lax.rem((INST - inst) * STREAM, LANES), 1)
    first = jnp.where(lane < STREAM, first, 0.0)
    step_lane = first + pltpu.roll(first, 32, 1) + pltpu.roll(first, 64, 1) + pltpu.roll(first, 96, 1)

    column = jnp.broadcast_to(partner_ref[0:1, :], (8, 8)).astype(F32)
    same = lax.broadcasted_iota(jnp.int32, (8, 8), 0) == lax.broadcasted_iota(jnp.int32, (8, 8), 1)
    column = jnp.sum(jnp.where(same, column, 0.0), axis=1, keepdims=True).astype(jnp.int32)
    ahead = lax.shift_right_arithmetic(jnp.broadcast_to(column, (8, LANES)), 2)
    behind = (2 * row + 128 - ahead) & 63

    wanted = tuple(
        jnp.concatenate([ahead[4 * side : 4 * side + 4], behind[4 * side : 4 * side + 4]], 0) for side in range(2)
    )

    t01_ref[...] = jnp.zeros_like(t01_ref)
    ct_ref[...] = jnp.zeros_like(ct_ref)
    tr_send[...] = jnp.zeros_like(tr_send)

    def unpack(side):
        for start in range(0, HALF, chunk):
            even = a_recv[2 * side, start : start + chunk, :]
            odd = a_recv[2 * side + 1, start : start + chunk, :]
            upper = jnp.where(lane < 64, even, pltpu.roll(odd, 64, 1))
            lower = jnp.where(lane < 64, pltpu.roll(even, 64, 1), odd)
            base_ref[side, start : start + chunk, :] = upper
            u_ref[side, start : start + chunk, :] = upper
            base_ref[side, HALF + start : HALF + start + chunk, :] = lower
            u_ref[side, HALF + start : HALF + start + chunk, :] = lower

    stream = lane & 31
    eighth = lax.broadcasted_iota(jnp.int32, (8, LANES), 0)
    own_tau = jnp.where(eighth < 4, step_lane[:, 15:16], step_lane[:, 16:17])
    near = lax.div(inst, 2)
    far = 1 - near

    def hop(buffer, k, side, sender, send_sem, recv_sem, device):
        return pltpu.make_async_remote_copy(
            src_ref=buffer.at[k, side, sender],
            dst_ref=buffer.at[k, side, sender],
            send_sem=send_sem,
            recv_sem=recv_sem.at[k, side],
            device_id=(inst, device),
            device_id_type=MESH,
        )

    def all_of(part, sem):
        pltpu.make_async_copy(part, part, sem).wait()

    def trace_copy(k, side, sent, landed, send_sem, recv_sem, device):
        return pltpu.make_async_remote_copy(
            src_ref=tr_send.at[k, side, sent],
            dst_ref=tr_recv.at[k, side, landed],
            send_sem=send_sem,
            recv_sem=recv_sem.at[k, side],
            device_id=device,
            device_id_type=MESH,
        )

    def upward(k, side):
        return trace_copy(k, side, 3, 2, us_sem, ur_sem, (lax.rem(inst + 1, INST), row))

    def downward(k, side):
        return trace_copy(k, side, 2, 3, ds_sem, dr_sem, (lax.rem(inst + INST - 1, INST), row))

    has_above = inst < INST - 1
    has_below = inst > 0

    def interior_traces(side):
        for var in range(5):
            t01_ref[0, side, var * 25 : var * 25 + 25, :] = u_ref[side, var * 128 : var * 128 + 25, :]
            t01_ref[1, side, var * 25 : var * 25 + 25, :] = u_ref[side, var * 128 + 100 : var * 128 + 125, :]

    def slide(k, side):
        ct_ref[0] = jnp.transpose(jnp.where(stream == 15, t01_ref[1, side], t01_ref[0, side]))
        slab = jnp.concatenate([ct_ref[0, pl.ds(15 + kind, 4, stride=32), :] for kind in range(2)], 0)
        zbuf[k, side, low] = jnp.where(lane == 125, own_tau, slab)
        for distance in (4, 3, 5, 2, 6, 1, 7):
            hop(zbuf, k, side, low, zs_sem, zr_sem, high * RING + low_peer(distance)).start()

    def send_traces(k, side):
        for var in range(5):
            for depth in range(5):
                for face in range(2):
                    tr_send[k, side, face, pl.ds(var * 25 + depth, 5, stride=5), :] = u_ref[
                        side, pl.ds(var * 128 + 20 * face + depth, 5, stride=25), :
                    ]
        trace_copy(k, side, 1, 0, ps_sem, pr_sem, (inst, north)).start()
        trace_copy(k, side, 0, 1, ps_sem, pr_sem, (inst, south)).start()
        for var in range(5):
            for face in range(2):
                tr_send[k, side, 2 + face, var * 25 : var * 25 + 25, :] = u_ref[
                    side, pl.ds(var * 128 + 4 * face, 25, stride=5), :
                ]

        @pl.when(has_above)
        def _():
            upward(k, side).start()

        @pl.when(has_below)
        def _():
            downward(k, side).start()

    def begin(side):
        unpack(side)
        interior_traces(side)
        slide(0, side)
        send_traces(0, side)

    arrival(a_recv, a_send, as_sem, ar_sem, partner_inst).wait_recv()
    begin(near)
    for peer in peers[:2]:
        arrival(a_recv, a_send, as_sem, ar_sem, peer).wait_recv()
    begin(far)

    def section_weight(k):
        return jnp.where(k == 0, 0.25, jnp.where(k == 1, 1.0 / 3.0, jnp.where(k == 2, 0.5, 1.0)))

    def pick(buffer, k, side, digit):
        wanted_here = jnp.where(side == 0, wanted[0], wanted[1])
        digits = wanted_here & 7 if digit == 0 else lax.shift_right_arithmetic(wanted_here, 3)
        picked = buffer[k, side, 0]
        for other in range(1, RING):
            picked = jnp.where(digits == other, buffer[k, side, other], picked)
        return picked

    def place(target, start, value):
        fine, rest = split(value)
        target[start : start + 128, :] = fine
        target[256 + start : 256 + start + 128, :] = rest
        target[512 + start : 512 + start + 128, :] = fine

    def give_back(targets, remote):
        for target, away in zip(targets, remote):
            side = lax.div(target, 2)
            turn = 64 * lax.rem(target, 2)
            for start in range(0, HALF, chunk):
                upper = pltpu.roll(u_ref[side, start : start + chunk, :], turn, 1)
                lower = pltpu.roll(u_ref[side, HALF + start : HALF + start + chunk, :], 64 - turn, 1)
                b_send[target, start : start + chunk, :] = jnp.where(lane < 64, upper, lower)
            if away:
                exchange(b_send, out_ref, bs_sem, br_sem, target).start()
            else:
                pltpu.make_async_copy(b_send.at[target], out_ref.at[target], own_sem).start()

    def stage(k, carry):
        leading = jnp.where(k == STAGES - 1, far, near)
        weight = section_weight(k)
        last = section_weight(k - 1)
        scale = weight * step_lane

        @pl.when(k > 0)
        def _():
            interior_traces(0)
            interior_traces(1)

        known = jnp.concatenate([seen_ref[0], mine_ref[0], seen_ref[1], mine_ref[1]], 0)
        through = [
            lax.dot_general(
                known, g_ref[face], (((1,), (1,)), ((), ())), precision=HIGHEST, preferred_element_type=F32
            )
            for face in range(2)
        ]
        for side in range(2):
            back = [
                jnp.concatenate([through[1][start + 4 : start + 8], through[0][start : start + 4]], 0)
                for start in (16 * side, 16 * side + 8)
            ]
            mine_ref[side] = zbuf[k, side, low] - (last * own_tau) * back[0]
            lag_ref[side] = (last * tau_ref[side]) * back[1]

        for side in range(2):
            here = slice(side * LANES, (side + 1) * LANES)
            fine, rest = split(u_ref[side])
            ru_ref[0:ROWS, here] = fine
            ru_ref[ROWS : 2 * ROWS, here] = rest
            ru_ref[2 * ROWS : 3 * ROWS, here] = fine
            west = jnp.where((stream == 0) | (stream == 16), 0.0, pltpu.roll(t01_ref[1, side], 1, 1))
            east = jnp.where((stream == 31) | (stream == 15), 0.0, pltpu.roll(t01_ref[0, side], 127, 1))
            for face, value in ((0, west), (1, east)):
                fine, rest = split(value - t01_ref[face, side])
                rb_ref[face * 128 : (face + 1) * 128, here] = fine
                rb_ref[256 + face * 128 : 256 + (face + 1) * 128, here] = rest
                rb_ref[512 + face * 128 : 512 + (face + 1) * 128, here] = fine

        def add(left, right, first=False):
            both = halves(left, right)
            for side in range(2):
                part = both[:, side * LANES : (side + 1) * LANES]
                if first:
                    r_ref[side] = part
                else:
                    r_ref[side] += part

        add(wk_ref, ru_ref, True)
        add(ru_ref.at[0:ROWS], sh_ref)
        add(ru_ref.at[ROWS : 2 * ROWS], sh_ref)
        add(ru_ref.at[0:ROWS], sl_ref)
        add(wb_ref, rb_ref)

        for side in (near, far):
            all_of(zbuf.at[k, side, pl.ds(0, RING - 1)], zr_sem.at[k, side])
            hbuf[k, side, high] = pick(zbuf, k, side, 0)
            for distance in (3, 5, 2, 6, 1, 7, 4):
                hop(hbuf, k, side, high, hs_sem, hr_sem, high_peer(distance) * RING + low).start()

        for side in (near, far):
            @pl.when(has_below)
            def _(side=side):
                upward(k, side).wait_recv()

            @pl.when(has_above)
            def _(side=side):
                downward(k, side).wait_recv()

            for face in range(2):
                place(ra_ref, face * 128, tr_recv[k, side, 2 + face] - tr_send[k, side, 2 + face])
            r_ref[side] += halves(wc_ref, ra_ref)
            all_of(tr_recv.at[k, side, pl.ds(0, 2)], pr_sem.at[k, side])
            for face in range(2):
                place(ra_ref, face * 128, tr_recv[k, side, face] - tr_send[k, side, face])
            total = r_ref[side] + halves(wa_ref, ra_ref)
            u_ref[side] = base_ref[side] - scale * total

            @pl.when(k < STAGES - 1)
            def _(side=side):
                interior_traces(side)
                slide(k + 1, side)

        for order, side in enumerate((leading, 1 - leading)):
            all_of(hbuf.at[k, side, pl.ds(0, RING - 1)], hr_sem.at[k, side])
            seen = pick(hbuf, k, side, 1)

            @pl.when(k == 0)
            def _(side=side, seen=seen):
                tau_ref[side] = jnp.broadcast_to(seen[:, 125:126], (8, LANES))

            seen = seen - lag_ref[side]
            seen_ref[side] = seen
            ct_ref[1, pl.ds(16, 4, stride=32), :] = seen[0:4]
            ct_ref[1, pl.ds(15, 4, stride=32), :] = seen[4:8]
            across = jnp.transpose(ct_ref[1])
            for face in range(2):
                place(ra_ref, face * 128, jnp.where(stream == 16 - face, across, 0.0))
            u_ref[side] -= scale * halves(wb_ref, ra_ref)

            @pl.when(k < STAGES - 1)
            def _(side=side):
                send_traces(k + 1, side)

            @pl.when(k == STAGES - 1)
            def _(order=order):
                if order == 0:
                    give_back(peers[:2], (True, True))
                else:
                    give_back(peers[2:], (True, False))
        return carry

    lax.fori_loop(0, STAGES, stage, 0)

    own = pltpu.make_async_copy(b_send.at[inst], out_ref.at[inst], own_sem)
    all_of(a_send.at[pl.ds(0, INST - 1)], as_sem)
    all_of(b_send.at[pl.ds(0, INST - 1)], bs_sem)
    all_of(zbuf.at[:, :, pl.ds(0, RING - 1)], zs_sem)
    all_of(hbuf.at[:, :, pl.ds(0, RING - 1)], hs_sem)
    all_of(tr_send.at[:, :, pl.ds(0, 2)], ps_sem)

    @pl.when(has_above)
    def _():
        all_of(tr_send.at[:, :, 3], us_sem)

    @pl.when(has_below)
    def _():
        all_of(tr_send.at[:, :, 2], ds_sem)

    own.wait()
    for peer in peers[:3]:
        arrival(out_ref, b_send, bs_sem, br_sem, peer).wait_recv()


def finish(parts_hbm, out_ref, parts_ref, x_ref, in_sem, out_sem):
    lane = lax.broadcasted_iota(jnp.int32, (1, LANES), 1)
    pieces = 4
    piece = HALF // pieces
    loads = [
        pltpu.make_async_copy(
            parts_hbm.at[:, pl.ds(part * piece, piece), :], parts_ref.at[:, pl.ds(part * piece, piece), :],
            in_sem.at[part],
        )
        for part in range(pieces)
    ]

    def runs(part):
        found = []
        for upper in range(2):
            first, end = upper * HALF + part * piece, upper * HALF + (part + 1) * piece
            while first < end:
                var, node = divmod(first, 128)
                stop = min(end, (var + 1) * 128)
                found.append((var, node, min(stop, var * 128 + 125) - first))
                first = stop
        return found

    for load in loads:
        load.start()
    for part in range(pieces):
        loads[part].wait()
        for start in range(part * piece, (part + 1) * piece, 40):
            parts = [parts_ref[source, start : start + 40, :] for source in range(INST)]
            for quarter in range(4):
                whole = None
                for source in range(INST):
                    turn = (STREAM * (source - quarter)) % LANES
                    moved = parts[source] if turn == 0 else pltpu.roll(parts[source], turn, 1)
                    whole = moved if whole is None else jnp.where(lane >= STREAM * source, moved, whole)
                begin = (quarter // 2) * HALF + start
                x_ref[quarter % 2, begin : begin + 40, :] = whole
        for var, node, count in runs(part):
            for half in range(2):
                pltpu.make_async_copy(
                    x_ref.at[half, pl.ds(var * 128 + node, count), :],
                    out_ref.at[var, pl.ds(node, count), half, :],
                    out_sem.at[part],
                ).start()
    for part in range(pieces):
        every = x_ref.at[0, pl.ds(0, 2 * sum(count for _, _, count in runs(part))), :]
        pltpu.make_async_copy(every, every, out_sem.at[part]).wait()


def per_device(
    flow_state, flux_matrices, derivative, penalty, lift_matrices, frequency, step_size, partner
):
    outside = pl.BlockSpec(memory_space=pltpu.HBM)
    dma = pltpu.SemaphoreType.DMA
    parts = pl.pallas_call(
        kernel,
        out_shape=jax.ShapeDtypeStruct((INST, HALF, LANES), F32),
        in_specs=[outside, outside, outside, outside, outside, outside, outside, outside],
        out_specs=outside,
        scratch_shapes=[
            pltpu.VMEM((5, 3, 5), F32),
            pltpu.VMEM((3, 125, 125), F32),
            pltpu.VMEM((5, 6, 5), F32),
            pltpu.VMEM((6, FACE, 125), F32),
            pltpu.VMEM((1, LANES), F32),
            pltpu.VMEM((4, 8), jnp.int32),
            pltpu.VMEM((1, 1), F32),
            pltpu.VMEM((2, 5, LANES, LANES), F32),
            pltpu.VMEM((INST, HALF, LANES), F32),
            pltpu.VMEM((INST, HALF, LANES), F32),
            pltpu.VMEM((INST, HALF, LANES), F32),
            pltpu.VMEM((2, ROWS, LANES), F32),
            pltpu.VMEM((2, ROWS, LANES), F32),
            pltpu.VMEM((3 * ROWS, 256), BF16),
            pltpu.VMEM((ROWS, 3 * ROWS), BF16),
            pltpu.VMEM((ROWS, 3 * 256), BF16),
            pltpu.VMEM((ROWS, 3 * 256), BF16),
            pltpu.VMEM((ROWS, 3 * 256), BF16),
            pltpu.VMEM((3 * 256, LANES), BF16),
            pltpu.VMEM((3 * 256, 256), BF16),
            pltpu.VMEM((256, 256), BF16),
            pltpu.VMEM((256, 256), BF16),
            pltpu.VMEM((2, ROWS, LANES), F32),
            pltpu.VMEM((STAGES, 2, 4, LANES, LANES), F32),
            pltpu.VMEM((STAGES, 2, 4, LANES, LANES), F32),
            pltpu.VMEM((2, 2, LANES, LANES), F32),
            pltpu.VMEM((STAGES, 2, RING, 8, LANES), F32),
            pltpu.VMEM((STAGES, 2, RING, 8, LANES), F32),
            pltpu.VMEM((3, LANES, LANES), F32),
            pltpu.VMEM((6, LANES, LANES), F32),
            pltpu.VMEM((6, 8, LANES), F32),
            pltpu.VMEM((2, LANES, LANES), F32),
            pltpu.VMEM((2, LANES, LANES), F32),
            pltpu.VMEM((2, 8, LANES), F32),
            pltpu.VMEM((2, 8, LANES), F32),
            pltpu.VMEM((2, 8, LANES), F32),
            pltpu.VMEM((2, 8, LANES), F32),
            dma((2,)),
            dma((7,)),
            dma,
            dma((INST,)),
            dma,
            dma((INST,)),
            dma,
            dma,
            dma,
            dma,
            dma,
            dma((STAGES, 2)),
            dma((STAGES, 2)),
            dma((STAGES, 2)),
            dma((STAGES, 2)),
            dma((STAGES, 2)),
            dma,
        ],
        compiler_params=pltpu.CompilerParams(
            collective_id=0, has_side_effects=True, vmem_limit_bytes=67_043_328
        ),
    )(
        jnp.transpose(flow_state, (1, 2, 0, 3)), jnp.transpose(flux_matrices, (1, 0, 2)), derivative,
        jnp.transpose(penalty, (1, 0, 2)), jnp.transpose(lift_matrices, (0, 2, 1)),
        frequency.reshape(1, 1),
        step_size.reshape(1, LANES), jnp.transpose(partner, (1, 0)),
    )
    result = pl.pallas_call(
        finish,
        out_shape=jax.ShapeDtypeStruct((5, 125, 2, LANES), F32),
        in_specs=[outside],
        out_specs=outside,
        scratch_shapes=[
            pltpu.VMEM((INST, HALF, LANES), F32),
            pltpu.VMEM((2, ROWS, LANES), F32),
            dma((4,)),
            dma((4,)),
        ],
        compiler_params=pltpu.CompilerParams(vmem_limit_bytes=67_043_328),
    )(parts)
    return jnp.transpose(result, (2, 0, 1, 3))


def solution(mesh):
    placed = (P("inst", None, None, "elem"), P(), P(), P(), P(), P(), P("elem"), P(None, "elem"))
    return jax.shard_map(
        per_device,
        mesh=mesh,
        in_specs=placed,
        out_specs=P("inst", None, None, "elem"),
        check_vma=False,
    )
```
